32 devices in a mesh: lat: 8 (over z, x), gz: 4 (over y, core).
Axes of the slice: x: 2, y: 2, z: 4, core: 2. Of those that a mesh axis runs over, the one named last changes fastest.
Arguments:
- tiles: float32 [8, 1280, 512], P('gz', 'lat'), may hold values from 0.1 to 4.5
- offsets: int32 [8], replicated, may hold values from -32 to 0
- taps_x: float32 [31], replicated, may hold values from 0.01 to 0.1
- taps_y: float32 [31], replicated, may hold values from 0.01 to 0.1
- taps_z: float32 [63], replicated, may hold values from 0.005 to 0.05
Outputs:
- deconvolved: float32 [8, 1024, 512], P('gz', 'lat')
The draws below stay inside these ranges and needn't reach their ends.
Inputs may be any that keep to these rules, and one draw needn't show every extreme that they name: Tile d's first row belongs at stitched row d * 128 + offsets[d].
All inputs are finite; a program needn't handle non-finite values.
Results may differ from the reference program's by a relative error of at most 0.0001.
Values sent between devices are 32-bit elements; how exact they have to be, the bound alone decides.
A program may use at most 64 MiB of HBM per device.

```python
import math
import jax
import jax.numpy as jnp
from jax import lax

X = 512
BRICK = 128
SPILL = 32
TAPS_XY = 31
TAPS_Z = 63
ITERS = 2
TILE_ROWS = 160
YROWS = 1024
PLANES = 8
N_LAT = 8


def log_uniform(key, shape, lower, upper):
    return jnp.exp(jax.random.uniform(key, shape, jnp.float32, math.log(lower), math.log(upper)))


def draw_tiles(key, part):
    total_rows = N_LAT * TILE_ROWS
    plane_ids = jnp.arange(PLANES, dtype=jnp.int32) // 4
    row_ids = jnp.arange(total_rows, dtype=jnp.int32) // 8
    col_ids = jnp.arange(X, dtype=jnp.int32) // 8
    coarse_rows = jnp.arange(total_rows, dtype=jnp.int32) // 32
    coarse_cols = jnp.arange(X, dtype=jnp.int32) // 64
    fine_grid = ((PLANES + 3) // 4, (total_rows + 7) // 8, (X + 7) // 8)
    coarse_grid = ((PLANES + 3) // 4, (total_rows + 31) // 32, (X + 63) // 64)
    keys = jax.random.split(key, 8)

    def spread_fine(values):
        return values[plane_ids][:, row_ids][:, :, col_ids]

    def spread_coarse(values):
        return values[plane_ids][:, coarse_rows][:, :, coarse_cols]
    share = 0.35
    bright_low, bright_high = (1.0, 3.5)
    radius_low, radius_high = (0.8, 2.0)
    level = spread_coarse(log_uniform(keys[6], coarse_grid, 0.2, 0.6))
    noise = log_uniform(keys[7], (PLANES, total_rows, X), 0.7, 1.4)
    centre_plane = spread_fine(jax.random.uniform(keys[0], fine_grid, jnp.float32, 0.5, 2.5))
    centre_row = spread_fine(jax.random.uniform(keys[1], fine_grid, jnp.float32, 1.5, 6.5))
    centre_col = spread_fine(jax.random.uniform(keys[2], fine_grid, jnp.float32, 1.5, 6.5))
    present = jax.random.uniform(keys[3], fine_grid, jnp.float32) < share
    brightness = jax.random.uniform(keys[4], fine_grid, jnp.float32, bright_low, bright_high)
    brightness = spread_fine(jnp.where(present, brightness, 0.0))
    radius = spread_fine(jax.random.uniform(keys[5], fine_grid, jnp.float32, radius_low, radius_high))
    local_plane = (jnp.arange(PLANES, dtype=jnp.int32) - plane_ids * 4).astype(jnp.float32)
    local_row = (jnp.arange(total_rows, dtype=jnp.int32) - row_ids * 8).astype(jnp.float32)
    local_col = (jnp.arange(X, dtype=jnp.int32) - col_ids * 8).astype(jnp.float32)
    delta_plane = local_plane[:, None, None] - centre_plane
    delta_row = local_row[None, :, None] - centre_row
    delta_col = local_col[None, None, :] - centre_col
    distance = delta_plane * delta_plane + delta_row * delta_row + delta_col * delta_col
    bead = brightness * jnp.exp(-distance / (2.0 * radius * radius))
    return (level * noise + bead).astype(jnp.float32)


def place_ends(result, rng, smallest, largest):
    longest = result.shape.index(max(result.shape))
    spots = []
    for shift in (0, 1):
        where = [jax.random.randint(jax.random.fold_in(rng, axis), (), 0, length) for axis, length in enumerate(result.shape)]
        where[longest] = (where[longest] + shift) % result.shape[longest]
        spots.append(tuple(where))
    return result.at[spots[0]].set(smallest).at[spots[1]].set(largest)


def setup_inputs(seed: int = 0) -> dict:
    streams_of = jax.random.split(jax.random.key(seed), 6)
    return {
        "tiles": draw_tiles(jax.random.fold_in(streams_of[5], 71), 0),
        "offsets": place_ends(jax.random.randint(streams_of[1], (N_LAT,), 0 - SPILL, 1), jax.random.fold_in(streams_of[1], 1), 0 - SPILL, 0).astype(jnp.int32),
        "taps_x": jnp.clip(jnp.exp(jax.random.uniform(streams_of[2], (TAPS_XY,), jnp.float32, math.log(0.01), math.log(0.1))), 0.01, 0.1),
        "taps_y": jnp.clip(jnp.exp(jax.random.uniform(streams_of[3], (TAPS_XY,), jnp.float32, math.log(0.01), math.log(0.1))), 0.01, 0.1),
        "taps_z": jnp.clip(jnp.exp(jax.random.uniform(streams_of[4], (TAPS_Z,), jnp.float32, math.log(0.005), math.log(0.05))), 0.005, 0.05),
    }


def band_matrix(taps, n_out, n_in, shift):
    reach = taps.shape[0] - 1
    offset = jnp.arange(n_in, dtype=jnp.int32)[None, :] - jnp.arange(n_out, dtype=jnp.int32)[:, None] + shift
    inside = (offset >= 0) & (offset <= reach)
    return jnp.where(inside, taps[jnp.clip(offset, 0, reach)], 0.0)


def along_x(volume, matrix):
    width = volume.shape[2]
    flat = jnp.dot(volume.reshape(-1, width), matrix, precision=lax.Precision.HIGHEST)
    return flat.reshape(volume.shape)


def along_z(volume, taps):
    half = (taps.shape[0] - 1) // 2
    depth = volume.shape[0]
    matrix = band_matrix(taps, depth, depth, half)
    flat = jnp.dot(matrix, volume.reshape(depth, -1), precision=lax.Precision.HIGHEST)
    return flat.reshape(volume.shape)


def along_y(volume, taps):
    reach = taps.shape[0] - 1
    half = reach // 2
    length = volume.shape[1]
    padded = jnp.pad(volume, ((0, 0), (half, half), (0, 0)))

    def add_tap(index, accum):
        return accum + taps[index] * lax.dynamic_slice_in_dim(padded, index, length, 1)

    return lax.fori_loop(0, reach + 1, add_tap, jnp.zeros_like(volume))


def stitch(tiles, offsets):
    accum = jnp.zeros((PLANES, YROWS + 2 * SPILL, X), tiles.dtype)
    counts = jnp.zeros((YROWS + 2 * SPILL,), tiles.dtype)

    def place(index, carry):
        accum, counts = carry
        begin = (index * BRICK + offsets[index] + SPILL).astype(jnp.int32)
        source = lax.dynamic_slice_in_dim(tiles, (index * TILE_ROWS).astype(jnp.int32), TILE_ROWS, 1)
        current = lax.dynamic_slice_in_dim(accum, begin, TILE_ROWS, 1)
        accum = lax.dynamic_update_slice_in_dim(accum, current + source, begin, 1)
        counted = lax.dynamic_slice_in_dim(counts, begin, TILE_ROWS, 0)
        counts = lax.dynamic_update_slice_in_dim(counts, counted + 1.0, begin, 0)
        return accum, counts

    accum, counts = lax.fori_loop(0, N_LAT, place, (accum, counts))
    return accum[:, SPILL:SPILL + YROWS] / counts[SPILL:SPILL + YROWS][None, :, None]


def reference(tiles, offsets, taps_x, taps_y, taps_z):
    observed = stitch(tiles, offsets)
    half = (taps_x.shape[0] - 1) // 2
    x_forward = band_matrix(taps_x, X, X, half).T
    x_adjoint = x_forward.T
    estimate = observed
    for step in range(ITERS):
        blurred = along_z(along_y(along_x(estimate, x_forward), taps_y), taps_z)
        ratio = observed / blurred
        back = along_x(along_y(along_z(ratio, taps_z[::-1]), taps_y[::-1]), x_adjoint)
        estimate = estimate * back
    return estimate
```

```python
import functools

import jax
import jax.numpy as jnp
from jax import lax
from jax.experimental import pallas as pl
from jax.experimental.pallas import tpu as pltpu
from jax.sharding import PartitionSpec as P

SPILL = 32
ITERS = 2
REACH = 16
CHUNKS = 2
LANES = 128
UNIT = 2 * REACH
VMEM_LIMIT = 60 * 1024 * 1024
MESH = pl.DeviceIdType.MESH
F32 = jnp.float32
BF16 = jnp.bfloat16


def halves(value):
    high = value.astype(BF16)
    return high, (value - high.astype(F32)).astype(BF16)


def product(left, right):
    (left_high, left_low), (right_high, right_low) = left, right

    def dot(a, b):
        return jnp.dot(a, b, preferred_element_type=F32)

    return dot(left_high, right_high) + (dot(left_high, right_low) + dot(left_low, right_high))


def banded(taps_ref, index):
    def add_tap(k, value):
        return jnp.where(index == k, taps_ref[k], value)

    return lax.fori_loop(0, taps_ref.shape[0], add_tap, jnp.zeros(index.shape, F32))


def shifted_rows(value, amount):
    length = value.shape[0]
    amounts = jnp.zeros(value.shape, jnp.int32) + amount
    bit = 1
    while bit <= SPILL:
        moved = pltpu.roll(value, length - bit, 0)
        value = jnp.where((amounts & bit) != 0, moved, value)
        bit *= 2
    return value[: length - SPILL]


def store_halves(ref, where, value):
    high, low = halves(value)
    ref[(0,) + where] = high
    ref[(1,) + where] = low


def kernel(
    lat_count, gz_count,
    tiles_hbm, offsets_hbm, taps_x_hbm, taps_y_hbm, taps_z_hbm, out_ref,
    tiles_ref, offsets_ref, taps_x_ref, taps_y_ref, taps_z_ref, load_sem,
    shifted, gathered, left_spill, right_spill, observed, estimate, ratio, lateral_y, final,
    x_forward, x_adjoint, yz_forward, yz_adjoint,
    tile_send, tile_recv, left_send, left_recv, right_send, right_recv,
    halo_send, halo_recv, final_send, final_recv, local_sem,
):
    lat, gz = lax.axis_index("lat"), lax.axis_index("gz")
    pairs = ((tiles_hbm, tiles_ref), (offsets_hbm, offsets_ref), (taps_x_hbm, taps_x_ref),
             (taps_y_hbm, taps_y_ref), (taps_z_hbm, taps_z_ref))
    loads = [pltpu.make_async_copy(source, target, load_sem.at[i])
             for i, (source, target) in enumerate(pairs)]
    for load in loads:
        load.start()
    plane_count, tile_rows, width = tiles_ref.shape
    slots, planes, rows, _ = observed.shape
    brick = tile_rows - SPILL
    depth = slots // 2
    spill_blocks = SPILL // rows
    units, _, unit, _ = ratio.shape
    out_rows = units * unit
    total = lat_count * gz_count

    chunk = width // CHUNKS
    chunks = [slice(c * chunk, (c + 1) * chunk) for c in range(CHUNKS)]

    def owner(lat_index, block):
        return jnp.where(lat_index % 2 == 0, block, gz_count - 1 - block)

    block = owner(lat, gz)
    place = lat * gz_count + block

    def device_at(position):
        lat_index = position // gz_count
        return lat_index, owner(lat_index, position % gz_count)

    own_planes = pl.ds(gz * plane_count, plane_count)

    def tile_copy(step, c):
        target = (gz + step) % gz_count
        source_rows = pl.ds(pl.multiple_of(owner(lat, target) * rows, rows), rows)
        return pltpu.make_async_remote_copy(
            shifted.at[:, source_rows, chunks[c]], gathered.at[own_planes, :, chunks[c]],
            tile_send.at[step, c], tile_recv.at[step, c], (lat, target), MESH)

    def right_going(q, c):
        return pltpu.make_async_remote_copy(
            tiles_ref.at[:, brick:tile_rows, chunks[c]],
            left_spill.at[own_planes, 0:SPILL, chunks[c]],
            left_send.at[q, c], left_recv.at[gz, c], (lat + 1, owner(lat + 1, q)), MESH)

    def left_going(q, c):
        return pltpu.make_async_remote_copy(
            tiles_ref.at[:, 0:SPILL, chunks[c]],
            right_spill.at[own_planes, SPILL:2 * SPILL, chunks[c]],
            right_send.at[q, c], right_recv.at[gz, c], (lat - 1, owner(lat - 1, gz_count - 1 - q)), MESH)

    has_right, has_left = lat < lat_count - 1, lat > 0
    others = [e for e in range(-depth, depth + 1) if e != 0]

    def there(e):
        return (place + e >= 0) & (place + e < total)

    barrier = pltpu.get_barrier_semaphore()

    def greet(device):
        pl.semaphore_signal(barrier, inc=1, device_id=device, device_id_type=MESH)

    expected = gz_count - 1 + jnp.where(has_right, spill_blocks, 0) + jnp.where(has_left, spill_blocks, 0)
    for step in range(1, gz_count):
        greet((lat, (gz + step) % gz_count))
    for e in others:
        expected = expected + jnp.where(there(e), 1, 0)

        @pl.when(there(e))
        def _():
            greet(device_at(place + e))

    @pl.when(has_left & (block < spill_blocks))
    def _():
        for source in range(gz_count):
            greet((lat - 1, source))

    @pl.when(has_right & (block >= gz_count - spill_blocks))
    def _():
        for source in range(gz_count):
            greet((lat + 1, source))

    loads[0].wait()
    loads[1].wait()
    own_offset = offsets_ref[lat]
    for plane in range(plane_count):
        shifted[plane] = shifted_rows(tiles_ref[plane], 0 - own_offset)
    pl.semaphore_wait(barrier, expected)

    for c in range(CHUNKS):
        @pl.when(has_right)
        def _():
            for q in range(spill_blocks):
                right_going(q, c).start()

        @pl.when(has_left)
        def _():
            for q in range(spill_blocks):
                left_going(q, c).start()

        for step in range(1, gz_count):
            tile_copy(step, c).start()
    own_rows = pl.ds(pl.multiple_of(block * rows, rows), rows)
    gathered[own_planes] = shifted[:, own_rows, :]

    @pl.when(has_left & (block < spill_blocks))
    def _():
        left_spill[:, SPILL:2 * SPILL, :] = jnp.zeros((planes, SPILL, width), F32)

    @pl.when(has_right & (block >= gz_count - spill_blocks))
    def _():
        right_spill[:, 0:SPILL, :] = jnp.zeros((planes, SPILL, width), F32)

    for e in others:
        @pl.when(jnp.logical_not(there(e)))
        def _():
            observed[depth + e] = jnp.zeros(observed.shape[1:], F32)
            estimate[depth + e] = jnp.zeros(estimate.shape[1:], F32)

    for load in loads[2:]:
        load.wait()
    half_xy = (taps_x_ref.shape[0] - 1) // 2
    half_z = (taps_z_ref.shape[0] - 1) // 2
    blocks = width // LANES
    gap = (lax.broadcasted_iota(jnp.int32, (LANES, LANES), 0)
           - lax.broadcasted_iota(jnp.int32, (LANES, LANES), 1))

    def build_x(matrix, sign):
        matrix[...] = jnp.zeros_like(matrix)
        for delta in (-1, 0, 1):
            value = banded(taps_x_ref, half_xy + sign * (gap + delta * LANES))
            for column in range(blocks):
                row = column + delta
                if 0 <= row < blocks:
                    spot = (slice(row * LANES, (row + 1) * LANES),
                            slice(column * LANES, (column + 1) * LANES))
                    store_halves(matrix, spot, value)

    build_x(x_forward, 1)

    def axial(lane_plane, plane, sign):
        weights = jnp.zeros(lane_plane.shape, F32)
        for other in range(planes):
            tap = taps_z_ref[half_z + sign * (other - plane)]
            weights = jnp.where(lane_plane == other, tap, weights)
        return weights

    lanes = lax.broadcasted_iota(jnp.int32, (out_rows, planes * rows), 1)
    out_ids = lax.broadcasted_iota(jnp.int32, (out_rows, planes * rows), 0)
    lane_row = lanes % rows
    lane_plane = (lax.broadcasted_iota(jnp.int32, (8, planes * rows), 1)) // rows

    def reached(slot):
        start = (slot - depth) * rows + REACH - half_xy
        return max(0, start // unit), min(units, (start + rows + 2 * half_xy - 1) // unit + 1)

    def build_axial(z, carry):
        weights = axial(lane_plane, z, 1)[0:1]
        for slot in range(slots):
            block_value = lateral_y[slot] * weights
            for u in range(*reached(slot)):
                spot = (slot, pl.ds(pl.multiple_of((u * planes + z) * unit, unit), unit), slice(None))
                store_halves(yz_forward, spot, block_value[u * unit:(u + 1) * unit])
        return carry

    for slot in range(slots):
        index = lane_row + (slot - depth) * rows - (out_ids - REACH) + half_xy
        lateral_y[slot] = banded(taps_y_ref, index)
    lax.fori_loop(0, planes, build_axial, 0)

    wide = planes * out_rows

    def build_adjoint():
        build_x(x_adjoint, -1)
        lane = lax.broadcasted_iota(jnp.int32, (rows, wide), 1)
        row_ids = lax.broadcasted_iota(jnp.int32, (rows, wide), 0)
        back_lateral = banded(taps_y_ref, half_xy - (lane // (unit * planes) * unit + lane % unit - REACH - row_ids))
        wide_plane = lax.broadcasted_iota(jnp.int32, (8, wide), 1) // unit % planes
        for z in range(planes):
            weights = axial(wide_plane, z, -1)[0:1]
            store_halves(yz_adjoint, (slice(z * rows, (z + 1) * rows), slice(None)), back_lateral * weights)

    left_offset = offsets_ref[jnp.maximum(lat - 1, 0)]
    right_offset = offsets_ref[jnp.minimum(lat + 1, lat_count - 1)]
    brick_rows = block * rows + lax.broadcasted_iota(jnp.int32, (rows, chunk), 0)
    from_left = has_left & (brick_rows < SPILL + left_offset)
    from_right = has_right & (brick_rows >= brick + right_offset)
    counts = 1.0 + jnp.where(from_left, 1.0, 0.0) + jnp.where(from_right, 1.0, 0.0)

    def halo_copy(buffer, which, e, c):
        return pltpu.make_async_remote_copy(
            buffer.at[depth, :, :, chunks[c]], buffer.at[depth - e, :, :, chunks[c]],
            halo_send.at[which, depth - e, c], halo_recv.at[which, depth - e, c],
            device_at(place + e), MESH)

    def send_halos(buffer, which, c):
        for e in others:
            @pl.when(there(e))
            def _():
                halo_copy(buffer, which, e, c).start()

    for c in range(CHUNKS):
        for step in range(1, gz_count):
            tile_copy(step, c).wait_recv()

        @pl.when(has_left & (block < spill_blocks))
        def _():
            for source in range(gz_count):
                sent = slice(source * plane_count, (source + 1) * plane_count)
                part = left_spill.at[sent, 0:SPILL, chunks[c]]
                pltpu.make_async_copy(part, part, left_recv.at[source, c]).wait()
            reach = pl.ds(pl.multiple_of(block * rows, 8), rows + SPILL)
            for z in range(planes):
                spill = left_spill[z, reach, chunks[c]]
                gathered[z, :, chunks[c]] += shifted_rows(spill, 0 - left_offset)

        @pl.when(has_right & (block >= gz_count - spill_blocks))
        def _():
            for source in range(gz_count):
                sent = slice(source * plane_count, (source + 1) * plane_count)
                part = right_spill.at[sent, SPILL:2 * SPILL, chunks[c]]
                pltpu.make_async_copy(part, part, right_recv.at[source, c]).wait()
            first = (block - (gz_count - spill_blocks)) * rows
            reach = pl.ds(pl.multiple_of(first, 8), rows + SPILL)
            for z in range(planes):
                spill = right_spill[z, reach, chunks[c]]
                gathered[z, :, chunks[c]] += shifted_rows(spill, 0 - right_offset)

        for z in range(planes):
            observed[depth, z, :, chunks[c]] = gathered[z, :, chunks[c]] / counts
        send_halos(observed, 0, c)

    build_adjoint()

    def final_copy(step, c):
        target = (gz + step) % gz_count
        return pltpu.make_async_remote_copy(
            final.at[pl.ds(target * plane_count, plane_count), :, chunks[c]],
            out_ref.at[:, own_rows, chunks[c]],
            final_send.at[step, c], final_recv.at[step, c], (lat, target), MESH)

    for which, buffer in zip(range(ITERS), [observed] + [estimate] * (ITERS - 1)):
        def part(slot, c):
            first, last = reached(slot)
            spot = slice(first * planes * unit, last * planes * unit)
            data = halves(buffer[slot, :, :, chunks[c]].reshape(planes * rows, chunk))
            value = product((yz_forward[0, slot, spot], yz_forward[1, slot, spot]), data)
            return {u: value[(u - first) * planes * unit:(u + 1 - first) * planes * unit]
                    for u in range(first, last)}

        sums = [part(depth, c) for c in range(CHUNKS)]
        blurred = None
        for c in range(CHUNKS):
            lateral = sums[c]
            for e in others:
                @pl.when(there(e))
                def _():
                    halo_copy(buffer, which, 0 - e, c).wait_recv()
                for u, value in part(depth + e, c).items():
                    lateral[u] = lateral[u] + value if u in lateral else value
            lateral = jnp.concatenate([lateral[u] for u in range(units)], 0)
            term = product(halves(lateral), (x_forward[0, chunks[c], :], x_forward[1, chunks[c], :]))
            blurred = term if blurred is None else blurred + term
        blurred = blurred.reshape(units, planes, unit, width)
        for u in range(units):
            row = u * unit - REACH + depth * rows
            slot, first = row // rows, row % rows
            quotient = observed[slot, :, first:first + unit, :] / blurred[u]
            ratio[u] = jnp.where(there(slot - depth), quotient, 0.0)
        data = halves(ratio[...].reshape(wide, width))
        back = halves(product((yz_adjoint[0], yz_adjoint[1]), data))
        for c in range(CHUNKS):
            gain = product(back, (x_adjoint[0, :, chunks[c]], x_adjoint[1, :, chunks[c]]))
            value = buffer[depth, :, :, chunks[c]] * gain.reshape(planes, rows, chunk)
            if which < ITERS - 1:
                estimate[depth, :, :, chunks[c]] = value
                send_halos(estimate, which + 1, c)
            else:
                final[:, :, chunks[c]] = value
                for step in range(1, gz_count):
                    final_copy(step, c).start()

    mine = pltpu.make_async_copy(final.at[own_planes], out_ref.at[:, own_rows, :], local_sem)
    mine.start()

    for c in range(CHUNKS):
        for step in range(1, gz_count):
            tile_copy(step, c).wait_send()

        @pl.when(has_right)
        def _():
            for q in range(spill_blocks):
                right_going(q, c).wait_send()

        @pl.when(has_left)
        def _():
            for q in range(spill_blocks):
                left_going(q, c).wait_send()

        for which, buffer in zip(range(ITERS), [observed] + [estimate] * (ITERS - 1)):
            for e in others:
                @pl.when(there(e))
                def _():
                    halo_copy(buffer, which, e, c).wait_send()

        for step in range(1, gz_count):
            final_copy(step, c).wait()
    mine.wait()


def by_rows(lat_count, gz_count, tiles, offsets, taps_x, taps_y, taps_z):
    plane_count, tile_rows, width = tiles.shape
    brick = tile_rows - SPILL
    rows = brick // gz_count
    planes = plane_count * gz_count
    depth = 2 * REACH // rows
    slots = 2 * depth + 1
    out_rows = rows + 2 * REACH
    unit = 16 if rows % 16 == 0 else 8
    spill_blocks = SPILL // rows
    dma = pltpu.SemaphoreType.DMA
    hbm = pl.BlockSpec(memory_space=pltpu.HBM)
    return pl.pallas_call(
        functools.partial(kernel, lat_count, gz_count),
        out_shape=jax.ShapeDtypeStruct((plane_count, brick, width), F32),
        in_specs=[hbm] * 5,
        out_specs=pl.BlockSpec(memory_space=pl.ANY),
        scratch_shapes=[
            pltpu.VMEM(tiles.shape, F32), pltpu.SMEM(offsets.shape, jnp.int32),
            pltpu.SMEM(taps_x.shape, F32), pltpu.SMEM(taps_y.shape, F32),
            pltpu.SMEM(taps_z.shape, F32), dma((5,)),
            pltpu.VMEM((plane_count, brick, width), F32),
            pltpu.VMEM((planes, rows, width), F32),
            pltpu.VMEM((planes, 2 * SPILL, width), F32),
            pltpu.VMEM((planes, 2 * SPILL, width), F32),
            pltpu.VMEM((slots, planes, rows, width), F32),
            pltpu.VMEM((slots, planes, rows, width), F32),
            pltpu.VMEM((out_rows // unit, planes, unit, width), F32),
            pltpu.VMEM((slots, out_rows, planes * rows), F32),
            pltpu.VMEM((planes, rows, width), F32),
            pltpu.VMEM((2, width, width), BF16),
            pltpu.VMEM((2, width, width), BF16),
            pltpu.VMEM((2, slots, planes * out_rows, planes * rows), BF16),
            pltpu.VMEM((2, planes * rows, planes * out_rows), BF16),
            dma((gz_count, CHUNKS)), dma((gz_count, CHUNKS)),
            dma((spill_blocks, CHUNKS)), dma((gz_count, CHUNKS)),
            dma((spill_blocks, CHUNKS)), dma((gz_count, CHUNKS)),
            dma((ITERS, slots, CHUNKS)), dma((ITERS, slots, CHUNKS)),
            dma((gz_count, CHUNKS)), dma((gz_count, CHUNKS)), dma,
        ],
        compiler_params=pltpu.CompilerParams(
            has_side_effects=True, collective_id=0, vmem_limit_bytes=60 * 1024 * 1024),
    )(tiles, offsets, taps_x, taps_y, taps_z)


def column_of(lane, outside):
    left, right = LANES + UNIT, LANES + 2 * UNIT
    return jnp.where(lane < LANES, lane,
                     jnp.where(lane < left, lane - left, jnp.where(lane < right, lane - UNIT, outside)))


def strip_kernel(
    lat_count, gz_count,
    tiles_hbm, offsets_hbm, taps_x_hbm, taps_y_hbm, taps_z_hbm, out_ref,
    tiles_ref, offsets_ref, taps_x_ref, taps_y_ref, taps_z_ref, load_sem,
    raw, spill_out, spill_in, observed, estimate, parts, quotient, edges, halo, final,
    x_forward, x_adjoint, yz_forward, yz_adjoint,
    tile_send, tile_recv, spill_send, spill_recv, row_send, row_recv,
    side_send, side_recv, final_send, final_recv,
):
    lat, gz = lax.axis_index("lat"), lax.axis_index("gz")
    pairs = ((tiles_hbm, tiles_ref), (offsets_hbm, offsets_ref), (taps_x_hbm, taps_x_ref),
             (taps_y_hbm, taps_y_ref), (taps_z_hbm, taps_z_ref))
    loads = [pltpu.make_async_copy(source, target, load_sem.at[i])
             for i, (source, target) in enumerate(pairs)]
    for load in loads:
        load.start()
    plane_count, tile_rows, width = tiles_ref.shape
    planes, brick, _ = final.shape
    blocks = brick // UNIT
    strips = gz_count
    groups = edges.shape[2]
    pack = planes // groups
    lane_x, core = lat % 2, gz % 2
    brick_id = lat - lane_x + core
    strip = jnp.where(lane_x == 0, gz // 2, strips - 1 - gz // 2)
    at_home = core == lane_x

    def device(brick_index, s):
        column = jnp.where(s < strips // 2, 0, 1)
        row = jnp.where(s < strips // 2, s, strips - 1 - s)
        return brick_index - brick_index % 2 + column, 2 * row + brick_index % 2

    has_up, has_down = brick_id > 0, brick_id < lat_count - 1
    has_left, has_right = strip > 0, strip < strips - 1
    vertical = {-1: has_up, 1: has_down}
    sideways = {-1: has_left, 1: has_right}

    def when(condition, action):
        pl.when(condition)(action)

    barrier = pltpu.get_barrier_semaphore()

    def greet(target):
        pl.semaphore_signal(barrier, inc=1, device_id=target, device_id_type=MESH)

    for step in range(1, 2 * gz_count):
        position = (lane_x * gz_count + gz + step) % (2 * gz_count)
        greet((lat - lane_x + position // gz_count, position % gz_count))
    expected = 2 * gz_count - 1
    outward = jnp.where(core == 0, -1, 1)
    has_outward = jnp.where(core == 0, brick_id, lat_count - 1 - brick_id) > 0
    for shift in (-1, 0, 1):
        condition = has_outward if shift == 0 else has_outward & sideways[shift]
        expected = expected + jnp.where(condition, 1, 0)
        when(condition, lambda shift=shift: greet(device(brick_id + outward, strip + shift)))

    side_rows = [slice(q * UNIT, (q + 1) * UNIT) for q in range(blocks + 2)]

    def clear_up():
        spill_in[0] = jnp.zeros(spill_in.shape[1:], F32)
        observed[:, side_rows[0], 0:LANES] = jnp.zeros((planes, UNIT, LANES), F32)
        estimate[:, :, side_rows[0], :] = jnp.zeros((ITERS - 1, planes, UNIT, LANES), F32)
        halo[:, :, :, side_rows[0], :] = jnp.zeros((ITERS, 2, groups, UNIT, LANES), F32)

    def clear_down():
        spill_in[1] = jnp.zeros(spill_in.shape[1:], F32)
        observed[:, side_rows[-1], 0:LANES] = jnp.zeros((planes, UNIT, LANES), F32)
        estimate[:, :, side_rows[-1], :] = jnp.zeros((ITERS - 1, planes, UNIT, LANES), F32)
        halo[:, :, :, side_rows[-1], :] = jnp.zeros((ITERS, 2, groups, UNIT, LANES), F32)

    def clear_side(side):
        halo[:, side] = jnp.zeros((ITERS, *halo.shape[2:]), F32)

    when(jnp.logical_not(has_up), clear_up)
    when(jnp.logical_not(has_down), clear_down)
    when(jnp.logical_not(has_left), lambda: clear_side(0))
    when(jnp.logical_not(has_right), lambda: clear_side(1))
    raw[:, 0:SPILL, :] = jnp.zeros((planes, SPILL, LANES), F32)
    raw[:, SPILL + tile_rows:, :] = jnp.zeros((planes, SPILL, LANES), F32)

    pieces = (slice(0, SPILL), slice(brick, tile_rows), slice(SPILL, brick))
    own_planes = pl.ds(gz * plane_count, plane_count)

    def lanes_of(s):
        return pl.ds(pl.multiple_of(s * LANES, LANES), LANES)

    def landed(piece):
        return slice(SPILL + piece.start, SPILL + piece.stop)

    def tile_copy(step, i):
        s = (strip + step) % strips
        return pltpu.make_async_remote_copy(
            tiles_ref.at[:, pieces[i], lanes_of(s)], raw.at[own_planes, landed(pieces[i]), :],
            tile_send.at[step, i], tile_recv.at[gz, i], device(lat, s), MESH)

    def tile_stay(i):
        return pltpu.make_async_copy(
            tiles_ref.at[:, pieces[i], lanes_of(strip)], raw.at[own_planes, landed(pieces[i]), :],
            tile_recv.at[gz, i])

    def arrived(part, semaphore):
        pltpu.make_async_copy(part, part, semaphore).wait()

    def tile_wait(i):
        for source in range(gz_count):
            sent = slice(source * plane_count, (source + 1) * plane_count)
            arrived(raw.at[sent, landed(pieces[i]), :], tile_recv.at[source, i])

    def send_tiles(steps, numbers):
        for i in numbers:
            for step in steps:
                if step > 0:
                    tile_copy(step, i).start()
                else:
                    when(at_home, lambda i=i: tile_stay(i).start())
                    when(jnp.logical_not(at_home), lambda i=i: tile_copy(0, i).start())

    loads[0].wait()
    pl.semaphore_wait(barrier, expected)
    send_tiles((*range(1, strips), 0), range(len(pieces)))

    for load in loads[1:]:
        load.wait()
    half_x = (taps_x_ref.shape[0] - 1) // 2
    half_y = (taps_y_ref.shape[0] - 1) // 2
    half_z = (taps_z_ref.shape[0] - 1) // 2
    far = 1 << 20

    def build_x(matrix, sign):
        _, depth, breadth = matrix.shape
        tall = LANES // 2
        for start in range(0, depth, tall):
            inner = start + lax.broadcasted_iota(jnp.int32, (tall, breadth), 0)
            outer = lax.broadcasted_iota(jnp.int32, (tall, breadth), 1)
            gap = column_of(inner, far) - column_of(outer, 0 - far)
            high, low = halves(banded(taps_x_ref, half_x + sign * gap))
            matrix[0, start:start + tall, :] = high
            matrix[1, start:start + tall, :] = low

    tall, deep = planes * UNIT, planes * 2 * UNIT

    def build_yz(matrix, sign):
        lane = lax.broadcasted_iota(jnp.int32, (UNIT, deep), 1)
        row = lax.broadcasted_iota(jnp.int32, (UNIT, deep), 0)
        lateral = banded(taps_y_ref, half_y + sign * (lane % (2 * UNIT) - row) - REACH * sign)
        lane_plane = lax.broadcasted_iota(jnp.int32, (8, deep), 1) // (2 * UNIT)
        for z in range(planes):
            weights = jnp.zeros(lane_plane.shape, F32)
            for other in range(planes):
                weights = jnp.where(lane_plane == other, taps_z_ref[half_z + sign * (other - z)], weights)
            high, low = halves(lateral * weights[0:1])
            matrix[z * UNIT:(z + 1) * UNIT, :] = high
            matrix[tall + z * UNIT:tall + (z + 1) * UNIT, :] = low

    build_x(x_forward, 1)
    build_yz(yz_forward, 1)

    own_offset = offsets_ref[brick_id]
    up_offset = offsets_ref[jnp.maximum(brick_id - 1, 0)]
    down_offset = offsets_ref[jnp.minimum(brick_id + 1, lat_count - 1)]

    def spill_copy(i):
        return pltpu.make_async_remote_copy(
            spill_out.at[i], spill_in.at[1 - i], spill_send.at[i], spill_recv.at[1 - i],
            device(brick_id + 2 * i - 1, strip), MESH)

    def placed(first):
        return [shifted_rows(raw[z, first:first + UNIT + SPILL, :], 0 - own_offset) for z in range(planes)]

    for i, condition in enumerate((has_up, has_down)):
        tile_wait(i)
        for z, value in enumerate(placed(i * (tile_rows))):
            spill_out[i, z] = value
        when(condition, lambda i=i: spill_copy(i).start())

    lane_ids = lax.broadcasted_iota(jnp.int32, (UNIT, LANES), 1)

    def current(which):
        return observed if which == 0 else estimate.at[which - 1]

    def row_copy(which, way):
        source = side_rows[1] if way < 0 else side_rows[blocks]
        target = side_rows[blocks + 1] if way < 0 else side_rows[0]
        i = (way + 1) // 2
        buffer = current(which)
        return pltpu.make_async_remote_copy(
            buffer.at[:, source, 0:LANES], buffer.at[:, target, 0:LANES],
            row_send.at[which, i], row_recv.at[which, i], device(brick_id + way, strip), MESH)

    def side_copy(which, shift, way, block):
        side = (1 - shift) // 2
        q = block + 1 if way == 0 else (blocks + 1 if way < 0 else 0)
        return pltpu.make_async_remote_copy(
            edges.at[which, side, :, block * UNIT:(block + 1) * UNIT, :],
            halo.at[which, side, :, side_rows[q], :],
            side_send.at[which, side, q], side_recv.at[which, side, q],
            device(brick_id + way, strip + shift), MESH)

    def all_copies(which, block):
        ways = ([-1] if block == 0 else []) + ([1] if block == blocks - 1 else [])
        copies = []
        for way in ways:
            for shift in (1, -1):
                copies.append((sideways[shift] & vertical[way], side_copy(which, shift, way, block)))
            copies.append((vertical[way], row_copy(which, way)))
        for shift in (1, -1):
            copies.append((sideways[shift], side_copy(which, shift, 0, block)))
        return copies

    def keep(which, block, values):
        rows = side_rows[block + 1]
        spot = slice(block * UNIT, (block + 1) * UNIT)
        buffer = current(which)
        for group in range(groups):
            right = left = None
            for j in range(pack):
                z = group * pack + j
                value = values[z]
                buffer[z, rows, 0:LANES] = value
                store_halves(parts.at[which], (z, rows, slice(0, LANES)), value)
                moved = pltpu.roll(value, (UNIT * (j + 1)) % LANES, 1) if j + 1 < pack else value
                right = moved if right is None else jnp.where(lane_ids // UNIT == j, moved, right)
                moved = pltpu.roll(value, UNIT * j, 1) if j > 0 else value
                left = moved if left is None else jnp.where(lane_ids // UNIT == j, moved, left)
            edges[which, 0, group, spot, :] = right
            edges[which, 1, group, spot, :] = left
        for condition, copy in all_copies(which, block):
            when(condition, lambda copy=copy: copy.start())

    def absorb(which, q):
        rows = side_rows[q]
        way = -1 if q == 0 else (1 if q == blocks + 1 else 0)
        buffer = current(which)
        if way != 0:
            when(vertical[way], lambda: arrived(buffer.at[:, rows, 0:LANES], row_recv.at[which, (1 - way) // 2]))
            for z in range(planes):
                store_halves(parts.at[which], (z, rows, slice(0, LANES)), buffer[z, rows, 0:LANES])
        for side, condition in enumerate((has_left, has_right)):
            condition = condition if way == 0 else condition & vertical[way]
            when(condition, lambda side=side: arrived(
                halo.at[which, side, :, rows, :], side_recv.at[which, side, q]))
        for group in range(groups):
            from_left, from_right = halo[which, 0, group, rows, :], halo[which, 1, group, rows, :]
            for j in range(pack):
                z = group * pack + j
                left = pltpu.roll(from_left, LANES - UNIT * j, 1) if j > 0 else from_left
                right = pltpu.roll(from_right, (LANES + UNIT - UNIT * j) % LANES, 1) if j != 1 else from_right
                value = jnp.where(lane_ids < UNIT, left, jnp.where(lane_ids < 2 * UNIT, right, 0.0))
                if which == 0:
                    observed[z, rows, LANES:2 * LANES] = value
                store_halves(parts.at[which], (z, rows, slice(LANES, 2 * LANES)), value)

    def dot(a, b):
        return jnp.dot(a, b, preferred_element_type=F32)

    def apply_yz(matrix, data_ref, first):
        high, low = [data_ref[i, :, first:first + 2 * UNIT, :].reshape(deep, 2 * LANES) for i in (0, 1)]
        both = dot(matrix[...], high)
        return both[:tall] + (both[tall:] + dot(matrix[:tall, :], low))

    def apply_x(value, matrix):
        high, low = halves(value)
        both = dot(jnp.concatenate([high, low], 0), matrix[0])
        return both[:tall] + (both[tall:] + dot(high, matrix[1]))

    wide_lane = lax.broadcasted_iota(jnp.int32, (UNIT, 2 * LANES), 1)
    wide_row = lax.broadcasted_iota(jnp.int32, (UNIT, 2 * LANES), 0)
    inside_columns = ((wide_lane < LANES)
                      | (has_left & (wide_lane >= LANES) & (wide_lane < LANES + UNIT))
                      | (has_right & (wide_lane >= LANES + UNIT) & (wide_lane < LANES + 2 * UNIT)))

    def forward(which, k):
        blurred = apply_x(apply_yz(yz_forward, parts.at[which], k * UNIT), x_forward)
        inside = inside_columns
        if k == 0:
            inside = inside & (has_up | (wide_row >= REACH))
        if k == blocks:
            inside = inside & (has_down | (wide_row < UNIT - REACH))
        for z in range(planes):
            start = k * UNIT + UNIT - REACH
            value = observed[z, start:start + UNIT, :] / blurred[z * UNIT:(z + 1) * UNIT]
            store_halves(quotient, (z, slice(k * UNIT, (k + 1) * UNIT), slice(None)),
                         jnp.where(inside, value, 0.0))

    def final_copy(step, block):
        target = (gz + step) % gz_count
        rows = slice(block * UNIT, (block + 1) * UNIT)
        return pltpu.make_async_remote_copy(
            final.at[pl.ds(target * plane_count, plane_count), rows, :],
            out_ref.at[:, rows, lanes_of(strip)],
            final_send.at[step, block], final_recv.at[strip, block], (brick_id, target), MESH)

    def final_stay(block):
        rows = slice(block * UNIT, (block + 1) * UNIT)
        return pltpu.make_async_copy(
            final.at[own_planes, rows, :], out_ref.at[:, rows, lanes_of(strip)], final_recv.at[strip, block])

    def adjoint(which, block):
        gain = apply_x(apply_yz(yz_adjoint, quotient, block * UNIT), x_adjoint)
        buffer = current(which)
        values = [buffer[z, side_rows[block + 1], 0:LANES] * gain[z * UNIT:(z + 1) * UNIT] for z in range(planes)]
        if which < ITERS - 1:
            keep(which + 1, block, values)
            return
        for z in range(planes):
            final[z, block * UNIT:(block + 1) * UNIT, :] = values[z]
        for step in range(1, gz_count):
            final_copy(step, block).start()
        when(at_home, lambda: final_stay(block).start())
        when(jnp.logical_not(at_home), lambda: final_copy(0, block).start())

    build_x(x_adjoint, -1)
    build_yz(yz_adjoint, -1)
    tile_wait(len(pieces) - 1)
    inner = list(range(1, blocks - 1))
    row_ids = lax.broadcasted_iota(jnp.int32, (UNIT, LANES), 0)

    def drain_tiles():
        for i in range(len(pieces)):
            for step in range(1, strips):
                tile_copy(step, i).wait_send()
            when(jnp.logical_not(at_home), lambda i=i: tile_copy(0, i).wait_send())
        for i, condition in enumerate((has_up, has_down)):
            when(condition, lambda i=i: spill_copy(i).wait_send())

    def drain_blocks(which):
        for block in range(blocks):
            for condition, copy in all_copies(which, block):
                when(condition, lambda copy=copy: copy.wait_send())

    def start_block(block):
        values = placed(SPILL + block * UNIT)
        for i, (edge, condition) in enumerate(((0, has_up), (blocks - 1, has_down))):
            if block == edge:
                when(condition, lambda i=i: arrived(spill_in.at[i], spill_recv.at[i]))
                limit = SPILL + up_offset - block * UNIT if i == 0 else brick + down_offset - block * UNIT
                shared = has_up & (row_ids < limit) if i == 0 else has_down & (row_ids >= limit)
                counts = jnp.where(shared, 2.0, 1.0)
                values = [(value + spill_in[i, z]) / counts for z, value in enumerate(values)]
        keep(0, block, values)

    start_block(1)
    start_block(2)
    start_block(0)
    start_block(3)
    drain_tiles()
    absorb(0, 2)
    absorb(0, 3)
    forward(0, 2)
    absorb(0, 1)
    forward(0, 1)
    adjoint(0, 1)
    absorb(0, 4)
    forward(0, 3)
    adjoint(0, 2)
    absorb(0, 0)
    forward(0, 0)
    adjoint(0, 0)
    absorb(0, 5)
    forward(0, 4)
    adjoint(0, 3)
    drain_blocks(0)
    absorb(1, 2)
    absorb(1, 3)
    forward(1, 2)
    absorb(1, 1)
    forward(1, 1)
    adjoint(1, 1)
    absorb(1, 4)
    forward(1, 3)
    adjoint(1, 2)
    absorb(1, 0)
    forward(1, 0)
    adjoint(1, 0)
    absorb(1, 5)
    forward(1, 4)
    adjoint(1, 3)
    drain_blocks(ITERS - 1)
    for s in range(strips):
        for block in range(blocks):
            part = out_ref.at[:, block * UNIT:(block + 1) * UNIT, s * LANES:(s + 1) * LANES]
            arrived(part, final_recv.at[s, block])
    for block in range(blocks):
        for step in range(1, gz_count):
            final_copy(step, block).wait_send()
        when(jnp.logical_not(at_home), lambda block=block: final_copy(0, block).wait_send())


def by_strips(lat_count, gz_count, tiles, offsets, taps_x, taps_y, taps_z):
    plane_count, tile_rows, width = tiles.shape
    brick = tile_rows - SPILL
    planes = plane_count * gz_count
    groups = planes // (LANES // UNIT)
    blocks = brick // UNIT
    tall, deep = planes * UNIT, planes * 2 * UNIT
    dma = pltpu.SemaphoreType.DMA
    hbm = pl.BlockSpec(memory_space=pltpu.HBM)
    return pl.pallas_call(
        functools.partial(strip_kernel, lat_count, gz_count),
        out_shape=jax.ShapeDtypeStruct((plane_count, brick, width), F32),
        in_specs=[hbm] * 5,
        out_specs=pl.BlockSpec(memory_space=pl.ANY),
        scratch_shapes=[
            pltpu.VMEM(tiles.shape, F32), pltpu.SMEM(offsets.shape, jnp.int32),
            pltpu.SMEM(taps_x.shape, F32), pltpu.SMEM(taps_y.shape, F32),
            pltpu.SMEM(taps_z.shape, F32), dma((5,)),
            pltpu.VMEM((planes, tile_rows + 2 * SPILL, LANES), F32),
            pltpu.VMEM((2, planes, SPILL, LANES), F32),
            pltpu.VMEM((2, planes, SPILL, LANES), F32),
            pltpu.VMEM((planes, brick + 2 * UNIT, 2 * LANES), F32),
            pltpu.VMEM((ITERS - 1, planes, brick + 2 * UNIT, LANES), F32),
            pltpu.VMEM((ITERS, 2, planes, brick + 2 * UNIT, 2 * LANES), BF16),
            pltpu.VMEM((2, planes, brick + UNIT, 2 * LANES), BF16),
            pltpu.VMEM((ITERS, 2, groups, brick, LANES), F32),
            pltpu.VMEM((ITERS, 2, groups, brick + 2 * UNIT, LANES), F32),
            pltpu.VMEM((planes, brick, LANES), F32),
            pltpu.VMEM((2, 2 * LANES, 2 * LANES), BF16),
            pltpu.VMEM((2, 2 * LANES, LANES), BF16),
            pltpu.VMEM((2 * tall, deep), BF16),
            pltpu.VMEM((2 * tall, deep), BF16),
            dma((gz_count, 3)), dma((gz_count, 3)), dma((2,)), dma((2,)),
            dma((ITERS, 2)), dma((ITERS, 2)),
            dma((ITERS, 2, blocks + 2)), dma((ITERS, 2, blocks + 2)),
            dma((gz_count, blocks)), dma((gz_count, blocks)),
        ],
        compiler_params=pltpu.CompilerParams(
            has_side_effects=True, collective_id=0, vmem_limit_bytes=VMEM_LIMIT),
    )(tiles, offsets, taps_x, taps_y, taps_z)


def local(lat_count, gz_count, tiles, offsets, taps_x, taps_y, taps_z):
    plane_count, tile_rows, width = tiles.shape
    brick, planes = tile_rows - SPILL, plane_count * gz_count
    fits = (width == gz_count * LANES and gz_count % 2 == 0 and lat_count % 2 == 0
            and planes % (LANES // UNIT) == 0 and brick % UNIT == 0 and brick >= 4 * UNIT)
    arrange = by_strips if fits else by_rows
    return arrange(lat_count, gz_count, tiles, offsets, taps_x, taps_y, taps_z)


def solution(mesh):
    in_specs = (P("gz", "lat", None), P(), P(), P(), P())
    out_specs = P("gz", "lat", None)
    body = functools.partial(local, mesh.shape["lat"], mesh.shape["gz"])
    return jax.shard_map(body, mesh=mesh, in_specs=in_specs, out_specs=out_specs, check_vma=False)
```

```python
import functools

import jax
import jax.numpy as jnp
from jax import lax
from jax.experimental import pallas as pl
from jax.experimental.pallas import tpu as pltpu
from jax.sharding import PartitionSpec as P

SPILL = 32
ITERS = 2
REACH = 16
CHUNKS = 2
LANES = 128
UNIT = 2 * REACH
VMEM_LIMIT = 60 * 1024 * 1024
MESH = pl.DeviceIdType.MESH
F32 = jnp.float32
BF16 = jnp.bfloat16


def halves(value):
    high = value.astype(BF16)
    return high, (value - high.astype(F32)).astype(BF16)


def product(left, right):
    (left_high, left_low), (right_high, right_low) = left, right

    def dot(a, b):
        return jnp.dot(a, b, preferred_element_type=F32)

    return dot(left_high, right_high) + (dot(left_high, right_low) + dot(left_low, right_high))


def banded(taps_ref, index):
    def add_tap(k, value):
        return jnp.where(index == k, taps_ref[k], value)

    return lax.fori_loop(0, taps_ref.shape[0], add_tap, jnp.zeros(index.shape, F32))


def shifted_rows(value, amount):
    length = value.shape[0]
    amounts = jnp.zeros(value.shape, jnp.int32) + amount
    bit = 1
    while bit <= SPILL:
        moved = pltpu.roll(value, length - bit, 0)
        value = jnp.where((amounts & bit) != 0, moved, value)
        bit *= 2
    return value[: length - SPILL]


def store_halves(ref, where, value):
    high, low = halves(value)
    ref[(0,) + where] = high
    ref[(1,) + where] = low


def kernel(
    lat_count, gz_count,
    tiles_hbm, offsets_hbm, taps_x_hbm, taps_y_hbm, taps_z_hbm, out_ref,
    tiles_ref, offsets_ref, taps_x_ref, taps_y_ref, taps_z_ref, load_sem,
    shifted, gathered, left_spill, right_spill, observed, estimate, ratio, lateral_y, final,
    x_forward, x_adjoint, yz_forward, yz_adjoint,
    tile_send, tile_recv, left_send, left_recv, right_send, right_recv,
    halo_send, halo_recv, final_send, final_recv, local_sem,
):
    lat, gz = lax.axis_index("lat"), lax.axis_index("gz")
    pairs = ((tiles_hbm, tiles_ref), (offsets_hbm, offsets_ref), (taps_x_hbm, taps_x_ref),
             (taps_y_hbm, taps_y_ref), (taps_z_hbm, taps_z_ref))
    loads = [pltpu.make_async_copy(source, target, load_sem.at[i])
             for i, (source, target) in enumerate(pairs)]
    for load in loads:
        load.start()
    plane_count, tile_rows, width = tiles_ref.shape
    slots, planes, rows, _ = observed.shape
    brick = tile_rows - SPILL
    depth = slots // 2
    spill_blocks = SPILL // rows
    units, _, unit, _ = ratio.shape
    out_rows = units * unit
    total = lat_count * gz_count

    chunk = width // CHUNKS
    chunks = [slice(c * chunk, (c + 1) * chunk) for c in range(CHUNKS)]

    def owner(lat_index, block):
        return jnp.where(lat_index % 2 == 0, block, gz_count - 1 - block)

    block = owner(lat, gz)
    place = lat * gz_count + block

    def device_at(position):
        lat_index = position // gz_count
        return lat_index, owner(lat_index, position % gz_count)

    own_planes = pl.ds(gz * plane_count, plane_count)

    def tile_copy(step, c):
        target = (gz + step) % gz_count
        source_rows = pl.ds(pl.multiple_of(owner(lat, target) * rows, rows), rows)
        return pltpu.make_async_remote_copy(
            shifted.at[:, source_rows, chunks[c]], gathered.at[own_planes, :, chunks[c]],
            tile_send.at[step, c], tile_recv.at[step, c], (lat, target), MESH)

    def right_going(q, c):
        return pltpu.make_async_remote_copy(
            tiles_ref.at[:, brick:tile_rows, chunks[c]],
            left_spill.at[own_planes, 0:SPILL, chunks[c]],
            left_send.at[q, c], left_recv.at[gz, c], (lat + 1, owner(lat + 1, q)), MESH)

    def left_going(q, c):
        return pltpu.make_async_remote_copy(
            tiles_ref.at[:, 0:SPILL, chunks[c]],
            right_spill.at[own_planes, SPILL:2 * SPILL, chunks[c]],
            right_send.at[q, c], right_recv.at[gz, c], (lat - 1, owner(lat - 1, gz_count - 1 - q)), MESH)

    has_right, has_left = lat < lat_count - 1, lat > 0
    others = [e for e in range(-depth, depth + 1) if e != 0]

    def there(e):
        return (place + e >= 0) & (place + e < total)

    barrier = pltpu.get_barrier_semaphore()

    def greet(device):
        pl.semaphore_signal(barrier, inc=1, device_id=device, device_id_type=MESH)

    expected = gz_count - 1 + jnp.where(has_right, spill_blocks, 0) + jnp.where(has_left, spill_blocks, 0)
    for step in range(1, gz_count):
        greet((lat, (gz + step) % gz_count))
    for e in others:
        expected = expected + jnp.where(there(e), 1, 0)

        @pl.when(there(e))
        def _():
            greet(device_at(place + e))

    @pl.when(has_left & (block < spill_blocks))
    def _():
        for source in range(gz_count):
            greet((lat - 1, source))

    @pl.when(has_right & (block >= gz_count - spill_blocks))
    def _():
        for source in range(gz_count):
            greet((lat + 1, source))

    loads[0].wait()
    loads[1].wait()
    own_offset = offsets_ref[lat]
    for plane in range(plane_count):
        shifted[plane] = shifted_rows(tiles_ref[plane], 0 - own_offset)
    pl.semaphore_wait(barrier, expected)

    for c in range(CHUNKS):
        @pl.when(has_right)
        def _():
            for q in range(spill_blocks):
                right_going(q, c).start()

        @pl.when(has_left)
        def _():
            for q in range(spill_blocks):
                left_going(q, c).start()

        for step in range(1, gz_count):
            tile_copy(step, c).start()
    own_rows = pl.ds(pl.multiple_of(block * rows, rows), rows)
    gathered[own_planes] = shifted[:, own_rows, :]

    @pl.when(has_left & (block < spill_blocks))
    def _():
        left_spill[:, SPILL:2 * SPILL, :] = jnp.zeros((planes, SPILL, width), F32)

    @pl.when(has_right & (block >= gz_count - spill_blocks))
    def _():
        right_spill[:, 0:SPILL, :] = jnp.zeros((planes, SPILL, width), F32)

    for e in others:
        @pl.when(jnp.logical_not(there(e)))
        def _():
            observed[depth + e] = jnp.zeros(observed.shape[1:], F32)
            estimate[depth + e] = jnp.zeros(estimate.shape[1:], F32)

    for load in loads[2:]:
        load.wait()
    half_xy = (taps_x_ref.shape[0] - 1) // 2
    half_z = (taps_z_ref.shape[0] - 1) // 2
    blocks = width // LANES
    gap = (lax.broadcasted_iota(jnp.int32, (LANES, LANES), 0)
           - lax.broadcasted_iota(jnp.int32, (LANES, LANES), 1))

    def build_x(matrix, sign):
        matrix[...] = jnp.zeros_like(matrix)
        for delta in (-1, 0, 1):
            value = banded(taps_x_ref, half_xy + sign * (gap + delta * LANES))
            for column in range(blocks):
                row = column + delta
                if 0 <= row < blocks:
                    spot = (slice(row * LANES, (row + 1) * LANES),
                            slice(column * LANES, (column + 1) * LANES))
                    store_halves(matrix, spot, value)

    build_x(x_forward, 1)

    def axial(lane_plane, plane, sign):
        weights = jnp.zeros(lane_plane.shape, F32)
        for other in range(planes):
            tap = taps_z_ref[half_z + sign * (other - plane)]
            weights = jnp.where(lane_plane == other, tap, weights)
        return weights

    lanes = lax.broadcasted_iota(jnp.int32, (out_rows, planes * rows), 1)
    out_ids = lax.broadcasted_iota(jnp.int32, (out_rows, planes * rows), 0)
    lane_row = lanes % rows
    lane_plane = (lax.broadcasted_iota(jnp.int32, (8, planes * rows), 1)) // rows

    def reached(slot):
        start = (slot - depth) * rows + REACH - half_xy
        return max(0, start // unit), min(units, (start + rows + 2 * half_xy - 1) // unit + 1)

    def build_axial(z, carry):
        weights = axial(lane_plane, z, 1)[0:1]
        for slot in range(slots):
            block_value = lateral_y[slot] * weights
            for u in range(*reached(slot)):
                spot = (slot, pl.ds(pl.multiple_of((u * planes + z) * unit, unit), unit), slice(None))
                store_halves(yz_forward, spot, block_value[u * unit:(u + 1) * unit])
        return carry

    for slot in range(slots):
        index = lane_row + (slot - depth) * rows - (out_ids - REACH) + half_xy
        lateral_y[slot] = banded(taps_y_ref, index)
    lax.fori_loop(0, planes, build_axial, 0)

    wide = planes * out_rows

    def build_adjoint():
        build_x(x_adjoint, -1)
        lane = lax.broadcasted_iota(jnp.int32, (rows, wide), 1)
        row_ids = lax.broadcasted_iota(jnp.int32, (rows, wide), 0)
        back_lateral = banded(taps_y_ref, half_xy - (lane // (unit * planes) * unit + lane % unit - REACH - row_ids))
        wide_plane = lax.broadcasted_iota(jnp.int32, (8, wide), 1) // unit % planes
        for z in range(planes):
            weights = axial(wide_plane, z, -1)[0:1]
            store_halves(yz_adjoint, (slice(z * rows, (z + 1) * rows), slice(None)), back_lateral * weights)

    left_offset = offsets_ref[jnp.maximum(lat - 1, 0)]
    right_offset = offsets_ref[jnp.minimum(lat + 1, lat_count - 1)]
    brick_rows = block * rows + lax.broadcasted_iota(jnp.int32, (rows, chunk), 0)
    from_left = has_left & (brick_rows < SPILL + left_offset)
    from_right = has_right & (brick_rows >= brick + right_offset)
    counts = 1.0 + jnp.where(from_left, 1.0, 0.0) + jnp.where(from_right, 1.0, 0.0)

    def halo_copy(buffer, which, e, c):
        return pltpu.make_async_remote_copy(
            buffer.at[depth, :, :, chunks[c]], buffer.at[depth - e, :, :, chunks[c]],
            halo_send.at[which, depth - e, c], halo_recv.at[which, depth - e, c],
            device_at(place + e), MESH)

    def send_halos(buffer, which, c):
        for e in others:
            @pl.when(there(e))
            def _():
                halo_copy(buffer, which, e, c).start()

    for c in range(CHUNKS):
        for step in range(1, gz_count):
            tile_copy(step, c).wait_recv()

        @pl.when(has_left & (block < spill_blocks))
        def _():
            for source in range(gz_count):
                sent = slice(source * plane_count, (source + 1) * plane_count)
                part = left_spill.at[sent, 0:SPILL, chunks[c]]
                pltpu.make_async_copy(part, part, left_recv.at[source, c]).wait()
            reach = pl.ds(pl.multiple_of(block * rows, 8), rows + SPILL)
            for z in range(planes):
                spill = left_spill[z, reach, chunks[c]]
                gathered[z, :, chunks[c]] += shifted_rows(spill, 0 - left_offset)

        @pl.when(has_right & (block >= gz_count - spill_blocks))
        def _():
            for source in range(gz_count):
                sent = slice(source * plane_count, (source + 1) * plane_count)
                part = right_spill.at[sent, SPILL:2 * SPILL, chunks[c]]
                pltpu.make_async_copy(part, part, right_recv.at[source, c]).wait()
            first = (block - (gz_count - spill_blocks)) * rows
            reach = pl.ds(pl.multiple_of(first, 8), rows + SPILL)
            for z in range(planes):
                spill = right_spill[z, reach, chunks[c]]
                gathered[z, :, chunks[c]] += shifted_rows(spill, 0 - right_offset)

        for z in range(planes):
            observed[depth, z, :, chunks[c]] = gathered[z, :, chunks[c]] / counts
        send_halos(observed, 0, c)

    build_adjoint()

    def final_copy(step, c):
        target = (gz + step) % gz_count
        return pltpu.make_async_remote_copy(
            final.at[pl.ds(target * plane_count, plane_count), :, chunks[c]],
            out_ref.at[:, own_rows, chunks[c]],
            final_send.at[step, c], final_recv.at[step, c], (lat, target), MESH)

    for which, buffer in zip(range(ITERS), [observed] + [estimate] * (ITERS - 1)):
        def part(slot, c):
            first, last = reached(slot)
            spot = slice(first * planes * unit, last * planes * unit)
            data = halves(buffer[slot, :, :, chunks[c]].reshape(planes * rows, chunk))
            value = product((yz_forward[0, slot, spot], yz_forward[1, slot, spot]), data)
            return {u: value[(u - first) * planes * unit:(u + 1 - first) * planes * unit]
                    for u in range(first, last)}

        sums = [part(depth, c) for c in range(CHUNKS)]
        blurred = None
        for c in range(CHUNKS):
            lateral = sums[c]
            for e in others:
                @pl.when(there(e))
                def _():
                    halo_copy(buffer, which, 0 - e, c).wait_recv()
                for u, value in part(depth + e, c).items():
                    lateral[u] = lateral[u] + value if u in lateral else value
            lateral = jnp.concatenate([lateral[u] for u in range(units)], 0)
            term = product(halves(lateral), (x_forward[0, chunks[c], :], x_forward[1, chunks[c], :]))
            blurred = term if blurred is None else blurred + term
        blurred = blurred.reshape(units, planes, unit, width)
        for u in range(units):
            row = u * unit - REACH + depth * rows
            slot, first = row // rows, row % rows
            quotient = observed[slot, :, first:first + unit, :] / blurred[u]
            ratio[u] = jnp.where(there(slot - depth), quotient, 0.0)
        data = halves(ratio[...].reshape(wide, width))
        back = halves(product((yz_adjoint[0], yz_adjoint[1]), data))
        for c in range(CHUNKS):
            gain = product(back, (x_adjoint[0, :, chunks[c]], x_adjoint[1, :, chunks[c]]))
            value = buffer[depth, :, :, chunks[c]] * gain.reshape(planes, rows, chunk)
            if which < ITERS - 1:
                estimate[depth, :, :, chunks[c]] = value
                send_halos(estimate, which + 1, c)
            else:
                final[:, :, chunks[c]] = value
                for step in range(1, gz_count):
                    final_copy(step, c).start()

    mine = pltpu.make_async_copy(final.at[own_planes], out_ref.at[:, own_rows, :], local_sem)
    mine.start()

    for c in range(CHUNKS):
        for step in range(1, gz_count):
            tile_copy(step, c).wait_send()

        @pl.when(has_right)
        def _():
            for q in range(spill_blocks):
                right_going(q, c).wait_send()

        @pl.when(has_left)
        def _():
            for q in range(spill_blocks):
                left_going(q, c).wait_send()

        for which, buffer in zip(range(ITERS), [observed] + [estimate] * (ITERS - 1)):
            for e in others:
                @pl.when(there(e))
                def _():
                    halo_copy(buffer, which, e, c).wait_send()

        for step in range(1, gz_count):
            final_copy(step, c).wait()
    mine.wait()


def by_rows(lat_count, gz_count, tiles, offsets, taps_x, taps_y, taps_z):
    plane_count, tile_rows, width = tiles.shape
    brick = tile_rows - SPILL
    rows = brick // gz_count
    planes = plane_count * gz_count
    depth = 2 * REACH // rows
    slots = 2 * depth + 1
    out_rows = rows + 2 * REACH
    unit = 16 if rows % 16 == 0 else 8
    spill_blocks = SPILL // rows
    dma = pltpu.SemaphoreType.DMA
    hbm = pl.BlockSpec(memory_space=pltpu.HBM)
    return pl.pallas_call(
        functools.partial(kernel, lat_count, gz_count),
        out_shape=jax.ShapeDtypeStruct((plane_count, brick, width), F32),
        in_specs=[hbm] * 5,
        out_specs=pl.BlockSpec(memory_space=pl.ANY),
        scratch_shapes=[
            pltpu.VMEM(tiles.shape, F32), pltpu.SMEM(offsets.shape, jnp.int32),
            pltpu.SMEM(taps_x.shape, F32), pltpu.SMEM(taps_y.shape, F32),
            pltpu.SMEM(taps_z.shape, F32), dma((5,)),
            pltpu.VMEM((plane_count, brick, width), F32),
            pltpu.VMEM((planes, rows, width), F32),
            pltpu.VMEM((planes, 2 * SPILL, width), F32),
            pltpu.VMEM((planes, 2 * SPILL, width), F32),
            pltpu.VMEM((slots, planes, rows, width), F32),
            pltpu.VMEM((slots, planes, rows, width), F32),
            pltpu.VMEM((out_rows // unit, planes, unit, width), F32),
            pltpu.VMEM((slots, out_rows, planes * rows), F32),
            pltpu.VMEM((planes, rows, width), F32),
            pltpu.VMEM((2, width, width), BF16),
            pltpu.VMEM((2, width, width), BF16),
            pltpu.VMEM((2, slots, planes * out_rows, planes * rows), BF16),
            pltpu.VMEM((2, planes * rows, planes * out_rows), BF16),
            dma((gz_count, CHUNKS)), dma((gz_count, CHUNKS)),
            dma((spill_blocks, CHUNKS)), dma((gz_count, CHUNKS)),
            dma((spill_blocks, CHUNKS)), dma((gz_count, CHUNKS)),
            dma((ITERS, slots, CHUNKS)), dma((ITERS, slots, CHUNKS)),
            dma((gz_count, CHUNKS)), dma((gz_count, CHUNKS)), dma,
        ],
        compiler_params=pltpu.CompilerParams(
            has_side_effects=True, collective_id=0, vmem_limit_bytes=60 * 1024 * 1024),
    )(tiles, offsets, taps_x, taps_y, taps_z)


def column_of(lane, outside):
    left, right = LANES + UNIT, LANES + 2 * UNIT
    return jnp.where(lane < LANES, lane,
                     jnp.where(lane < left, lane - left, jnp.where(lane < right, lane - UNIT, outside)))


def strip_kernel(
    lat_count, gz_count,
    tiles_hbm, offsets_hbm, taps_x_hbm, taps_y_hbm, taps_z_hbm, out_ref,
    tiles_ref, offsets_ref, taps_x_ref, taps_y_ref, taps_z_ref, load_sem,
    raw, spill_out, spill_in, observed, estimate, parts, middle, quotient, edges, halo, final,
    x_forward, x_adjoint, yz_forward, yz_adjoint,
    tile_send, tile_recv, spill_send, spill_recv, row_send, row_recv,
    side_send, side_recv, final_send, final_recv,
):
    lat, gz = lax.axis_index("lat"), lax.axis_index("gz")
    pairs = ((tiles_hbm, tiles_ref), (offsets_hbm, offsets_ref), (taps_x_hbm, taps_x_ref),
             (taps_y_hbm, taps_y_ref), (taps_z_hbm, taps_z_ref))
    loads = [pltpu.make_async_copy(source, target, load_sem.at[i])
             for i, (source, target) in enumerate(pairs)]
    for load in loads:
        load.start()
    plane_count, tile_rows, width = tiles_ref.shape
    planes, brick, _ = final.shape
    blocks = brick // UNIT
    strips = gz_count
    groups = edges.shape[2]
    pack = planes // groups
    lane_x, core = lat % 2, gz % 2
    brick_id = lat - lane_x + core
    strip = jnp.where(lane_x == 0, gz // 2, strips - 1 - gz // 2)
    at_home = core == lane_x

    def device(brick_index, s):
        column = jnp.where(s < strips // 2, 0, 1)
        row = jnp.where(s < strips // 2, s, strips - 1 - s)
        return brick_index - brick_index % 2 + column, 2 * row + brick_index % 2

    has_up, has_down = brick_id > 0, brick_id < lat_count - 1
    has_left, has_right = strip > 0, strip < strips - 1
    vertical = {-1: has_up, 1: has_down}
    sideways = {-1: has_left, 1: has_right}

    def when(condition, action):
        pl.when(condition)(action)

    barrier = pltpu.get_barrier_semaphore()

    def greet(target):
        pl.semaphore_signal(barrier, inc=1, device_id=target, device_id_type=MESH)

    for step in range(1, 2 * gz_count):
        position = (lane_x * gz_count + gz + step) % (2 * gz_count)
        greet((lat - lane_x + position // gz_count, position % gz_count))
    expected = 2 * gz_count - 1
    outward = jnp.where(core == 0, -1, 1)
    has_outward = jnp.where(core == 0, brick_id, lat_count - 1 - brick_id) > 0
    for shift in (-1, 0, 1):
        condition = has_outward if shift == 0 else has_outward & sideways[shift]
        expected = expected + jnp.where(condition, 1, 0)
        when(condition, lambda shift=shift: greet(device(brick_id + outward, strip + shift)))

    side_rows = [slice(q * UNIT, (q + 1) * UNIT) for q in range(blocks + 2)]

    def clear_up():
        spill_in[0] = jnp.zeros(spill_in.shape[1:], F32)
        observed[:, side_rows[0], 0:LANES] = jnp.zeros((planes, UNIT, LANES), F32)
        estimate[:, :, side_rows[0], :] = jnp.zeros((ITERS - 1, planes, UNIT, LANES), F32)
        halo[:, :, :, side_rows[0], :] = jnp.zeros((ITERS, 2, groups, UNIT, LANES), F32)

    def clear_down():
        spill_in[1] = jnp.zeros(spill_in.shape[1:], F32)
        observed[:, side_rows[-1], 0:LANES] = jnp.zeros((planes, UNIT, LANES), F32)
        estimate[:, :, side_rows[-1], :] = jnp.zeros((ITERS - 1, planes, UNIT, LANES), F32)
        halo[:, :, :, side_rows[-1], :] = jnp.zeros((ITERS, 2, groups, UNIT, LANES), F32)

    def clear_side(side):
        halo[:, side] = jnp.zeros((ITERS, *halo.shape[2:]), F32)

    when(jnp.logical_not(has_up), clear_up)
    when(jnp.logical_not(has_down), clear_down)
    when(jnp.logical_not(has_left), lambda: clear_side(0))
    when(jnp.logical_not(has_right), lambda: clear_side(1))
    raw[:, 0:SPILL, :] = jnp.zeros((planes, SPILL, LANES), F32)
    raw[:, SPILL + tile_rows:, :] = jnp.zeros((planes, SPILL, LANES), F32)

    pieces = (slice(0, SPILL), slice(brick, tile_rows), slice(SPILL, brick))
    own_planes = pl.ds(gz * plane_count, plane_count)

    def lanes_of(s):
        return pl.ds(pl.multiple_of(s * LANES, LANES), LANES)

    def landed(piece):
        return slice(SPILL + piece.start, SPILL + piece.stop)

    def tile_copy(step, i):
        s = (strip + step) % strips
        return pltpu.make_async_remote_copy(
            tiles_ref.at[:, pieces[i], lanes_of(s)], raw.at[own_planes, landed(pieces[i]), :],
            tile_send.at[step, i], tile_recv.at[gz, i], device(lat, s), MESH)

    def tile_stay(i):
        return pltpu.make_async_copy(
            tiles_ref.at[:, pieces[i], lanes_of(strip)], raw.at[own_planes, landed(pieces[i]), :],
            tile_recv.at[gz, i])

    def arrived(part, semaphore):
        pltpu.make_async_copy(part, part, semaphore).wait()

    def tile_wait(i):
        for source in range(gz_count):
            sent = slice(source * plane_count, (source + 1) * plane_count)
            arrived(raw.at[sent, landed(pieces[i]), :], tile_recv.at[source, i])

    def send_tiles(steps, numbers):
        for i in numbers:
            for step in steps:
                if step > 0:
                    tile_copy(step, i).start()
                else:
                    when(at_home, lambda i=i: tile_stay(i).start())
                    when(jnp.logical_not(at_home), lambda i=i: tile_copy(0, i).start())

    loads[0].wait()
    pl.semaphore_wait(barrier, expected)
    send_tiles((*range(1, strips), 0), range(len(pieces)))

    for load in loads[1:]:
        load.wait()
    half_x = (taps_x_ref.shape[0] - 1) // 2
    half_y = (taps_y_ref.shape[0] - 1) // 2
    half_z = (taps_z_ref.shape[0] - 1) // 2
    far = 1 << 20

    def build_x(matrix, sign):
        _, depth, breadth = matrix.shape
        tall = LANES // 2
        for start in range(0, depth, tall):
            inner = start + lax.broadcasted_iota(jnp.int32, (tall, breadth), 0)
            outer = lax.broadcasted_iota(jnp.int32, (tall, breadth), 1)
            gap = column_of(inner, far) - column_of(outer, 0 - far)
            high, low = halves(banded(taps_x_ref, half_x + sign * gap))
            matrix[0, start:start + tall, :] = high
            matrix[1, start:start + tall, :] = low

    tall, deep = planes * UNIT, planes * 2 * UNIT

    def build_yz(matrix, sign):
        lane = lax.broadcasted_iota(jnp.int32, (UNIT, deep), 1)
        row = lax.broadcasted_iota(jnp.int32, (UNIT, deep), 0)
        lateral = banded(taps_y_ref, half_y + sign * (lane % (2 * UNIT) - row) - REACH * sign)
        lane_plane = lax.broadcasted_iota(jnp.int32, (8, deep), 1) // (2 * UNIT)
        for z in range(planes):
            weights = jnp.zeros(lane_plane.shape, F32)
            for other in range(planes):
                weights = jnp.where(lane_plane == other, taps_z_ref[half_z + sign * (other - z)], weights)
            high, low = halves(lateral * weights[0:1])
            matrix[z * UNIT:(z + 1) * UNIT, :] = high
            matrix[tall + z * UNIT:tall + (z + 1) * UNIT, :] = low

    build_x(x_forward, 1)
    build_yz(yz_forward, 1)

    own_offset = offsets_ref[brick_id]
    up_offset = offsets_ref[jnp.maximum(brick_id - 1, 0)]
    down_offset = offsets_ref[jnp.minimum(brick_id + 1, lat_count - 1)]

    def spill_copy(i):
        return pltpu.make_async_remote_copy(
            spill_out.at[i], spill_in.at[1 - i], spill_send.at[i], spill_recv.at[1 - i],
            device(brick_id + 2 * i - 1, strip), MESH)

    def placed(first):
        return [shifted_rows(raw[z, first:first + UNIT + SPILL, :], 0 - own_offset) for z in range(planes)]

    for i, condition in enumerate((has_up, has_down)):
        tile_wait(i)
        for z, value in enumerate(placed(i * (tile_rows))):
            spill_out[i, z] = value
        when(condition, lambda i=i: spill_copy(i).start())

    lane_ids = lax.broadcasted_iota(jnp.int32, (UNIT, LANES), 1)

    def current(which):
        return observed if which == 0 else estimate.at[which - 1]

    def row_copy(which, way):
        source = side_rows[1] if way < 0 else side_rows[blocks]
        target = side_rows[blocks + 1] if way < 0 else side_rows[0]
        i = (way + 1) // 2
        buffer = current(which)
        return pltpu.make_async_remote_copy(
            buffer.at[:, source, 0:LANES], buffer.at[:, target, 0:LANES],
            row_send.at[which, i], row_recv.at[which, i], device(brick_id + way, strip), MESH)

    def side_copy(which, shift, way, block):
        side = (1 - shift) // 2
        q = block + 1 if way == 0 else (blocks + 1 if way < 0 else 0)
        return pltpu.make_async_remote_copy(
            edges.at[which, side, :, block * UNIT:(block + 1) * UNIT, :],
            halo.at[which, side, :, side_rows[q], :],
            side_send.at[which, side, q], side_recv.at[which, side, q],
            device(brick_id + way, strip + shift), MESH)

    def all_copies(which, block):
        ways = ([-1] if block == 0 else []) + ([1] if block == blocks - 1 else [])
        copies = []
        for way in ways:
            for shift in (1, -1):
                copies.append((sideways[shift] & vertical[way], side_copy(which, shift, way, block)))
            copies.append((vertical[way], row_copy(which, way)))
        for shift in (1, -1):
            copies.append((sideways[shift], side_copy(which, shift, 0, block)))
        return copies

    def keep(which, block, values):
        rows = side_rows[block + 1]
        spot = slice(block * UNIT, (block + 1) * UNIT)
        buffer = current(which)
        for group in range(groups):
            right = left = None
            for j in range(pack):
                z = group * pack + j
                value = values[z]
                buffer[z, rows, 0:LANES] = value
                store_halves(parts.at[which], (z, rows, slice(0, LANES)), value)
                moved = pltpu.roll(value, (UNIT * (j + 1)) % LANES, 1) if j + 1 < pack else value
                right = moved if right is None else jnp.where(lane_ids // UNIT == j, moved, right)
                moved = pltpu.roll(value, UNIT * j, 1) if j > 0 else value
                left = moved if left is None else jnp.where(lane_ids // UNIT == j, moved, left)
            edges[which, 0, group, spot, :] = right
            edges[which, 1, group, spot, :] = left

    def send_block(which, block):
        for condition, copy in all_copies(which, block):
            when(condition, lambda copy=copy: copy.start())

    def absorb(which, q):
        rows = side_rows[q]
        way = -1 if q == 0 else (1 if q == blocks + 1 else 0)
        buffer = current(which)
        if way != 0:
            when(vertical[way], lambda: arrived(buffer.at[:, rows, 0:LANES], row_recv.at[which, (1 - way) // 2]))
            for z in range(planes):
                store_halves(parts.at[which], (z, rows, slice(0, LANES)), buffer[z, rows, 0:LANES])
        for side, condition in enumerate((has_left, has_right)):
            condition = condition if way == 0 else condition & vertical[way]
            when(condition, lambda side=side: arrived(
                halo.at[which, side, :, rows, :], side_recv.at[which, side, q]))
        for group in range(groups):
            from_left, from_right = halo[which, 0, group, rows, :], halo[which, 1, group, rows, :]
            for j in range(pack):
                z = group * pack + j
                left = pltpu.roll(from_left, LANES - UNIT * j, 1) if j > 0 else from_left
                right = pltpu.roll(from_right, (LANES + UNIT - UNIT * j) % LANES, 1) if j != 1 else from_right
                value = jnp.where(lane_ids < UNIT, left, jnp.where(lane_ids < 2 * UNIT, right, 0.0))
                if which == 0:
                    observed[z, rows, LANES:2 * LANES] = value
                store_halves(parts.at[which], (z, rows, slice(LANES, 2 * LANES)), value)

    def dot(a, b):
        return jnp.dot(a, b, preferred_element_type=F32)

    def apply_yz(matrix, data_ref, first, slot):
        high, low = [data_ref[i, :, first:first + 2 * UNIT, :].reshape(deep, 2 * LANES) for i in (0, 1)]
        both = dot(matrix[...], high)
        value = both[:tall] + (both[tall:] + dot(matrix[:tall, :], low))
        middle[slot, :tall, :], middle[slot, tall:, :] = halves(value)

    def apply_x(matrix, slot):
        both = dot(middle[slot], matrix[0])
        return both[:tall] + (both[tall:] + dot(middle[slot, :tall, :], matrix[1]))

    wide_lane = lax.broadcasted_iota(jnp.int32, (UNIT, 2 * LANES), 1)
    wide_row = lax.broadcasted_iota(jnp.int32, (UNIT, 2 * LANES), 0)
    inside_columns = ((wide_lane < LANES)
                      | (has_left & (wide_lane >= LANES) & (wide_lane < LANES + UNIT))
                      | (has_right & (wide_lane >= LANES + UNIT) & (wide_lane < LANES + 2 * UNIT)))

    def forward_yz(which, k, slot):
        apply_yz(yz_forward, parts.at[which], k * UNIT, slot)

    def forward_x(which, k, slot):
        blurred = apply_x(x_forward, slot)
        inside = inside_columns
        if k == 0:
            inside = inside & (has_up | (wide_row >= REACH))
        if k == blocks:
            inside = inside & (has_down | (wide_row < UNIT - REACH))
        for z in range(planes):
            start = k * UNIT + UNIT - REACH
            value = observed[z, start:start + UNIT, :] / blurred[z * UNIT:(z + 1) * UNIT]
            store_halves(quotient, (z, slice(k * UNIT, (k + 1) * UNIT), slice(None)),
                         jnp.where(inside, value, 0.0))

    def final_copy(step, block):
        target = (gz + step) % gz_count
        rows = slice(block * UNIT, (block + 1) * UNIT)
        return pltpu.make_async_remote_copy(
            final.at[pl.ds(target * plane_count, plane_count), rows, :],
            out_ref.at[:, rows, lanes_of(strip)],
            final_send.at[step, block], final_recv.at[strip, block], (brick_id, target), MESH)

    def final_stay(block):
        rows = slice(block * UNIT, (block + 1) * UNIT)
        return pltpu.make_async_copy(
            final.at[own_planes, rows, :], out_ref.at[:, rows, lanes_of(strip)], final_recv.at[strip, block])

    def adjoint_yz(which, block, slot):
        apply_yz(yz_adjoint, quotient, block * UNIT, slot)

    def adjoint_x(which, block, slot):
        gain = apply_x(x_adjoint, slot)
        buffer = current(which)
        values = [buffer[z, side_rows[block + 1], 0:LANES] * gain[z * UNIT:(z + 1) * UNIT] for z in range(planes)]
        if which < ITERS - 1:
            keep(which + 1, block, values)
            return
        for z in range(planes):
            final[z, block * UNIT:(block + 1) * UNIT, :] = values[z]

    def send_result(which, block):
        if which < ITERS - 1:
            send_block(which + 1, block)
            return
        for step in range(1, gz_count):
            final_copy(step, block).start()
        when(at_home, lambda: final_stay(block).start())
        when(jnp.logical_not(at_home), lambda: final_copy(0, block).start())

    build_x(x_adjoint, -1)
    build_yz(yz_adjoint, -1)
    tile_wait(len(pieces) - 1)
    inner = list(range(1, blocks - 1))
    row_ids = lax.broadcasted_iota(jnp.int32, (UNIT, LANES), 0)

    def drain_tiles():
        for i in range(len(pieces)):
            for step in range(1, strips):
                tile_copy(step, i).wait_send()
            when(jnp.logical_not(at_home), lambda i=i: tile_copy(0, i).wait_send())
        for i, condition in enumerate((has_up, has_down)):
            when(condition, lambda i=i: spill_copy(i).wait_send())

    def drain_blocks(which):
        for block in range(blocks):
            for condition, copy in all_copies(which, block):
                when(condition, lambda copy=copy: copy.wait_send())

    def start_block(block):
        values = placed(SPILL + block * UNIT)
        for i, (edge, condition) in enumerate(((0, has_up), (blocks - 1, has_down))):
            if block == edge:
                when(condition, lambda i=i: arrived(spill_in.at[i], spill_recv.at[i]))
                limit = SPILL + up_offset - block * UNIT if i == 0 else brick + down_offset - block * UNIT
                shared = has_up & (row_ids < limit) if i == 0 else has_down & (row_ids >= limit)
                counts = jnp.where(shared, 2.0, 1.0)
                values = [(value + spill_in[i, z]) / counts for z, value in enumerate(values)]
        keep(0, block, values)
        send_block(0, block)

    start_block(1)
    start_block(2)
    start_block(0)
    start_block(3)
    drain_tiles()
    absorb(0, 2)
    absorb(0, 3)
    absorb(0, 1)
    absorb(0, 4)
    forward_yz(0, 2, 0)
    forward_yz(0, 1, 1)
    forward_x(0, 2, 0)
    forward_yz(0, 3, 0)
    forward_x(0, 1, 1)
    adjoint_yz(0, 1, 2)
    forward_x(0, 3, 0)
    adjoint_yz(0, 2, 3)
    adjoint_x(0, 1, 2)
    adjoint_x(0, 2, 3)
    send_result(0, 1)
    send_result(0, 2)
    absorb(0, 0)
    absorb(0, 5)
    forward_yz(0, 0, 1)
    forward_yz(0, 4, 0)
    forward_x(0, 0, 1)
    forward_x(0, 4, 0)
    adjoint_yz(0, 0, 2)
    adjoint_yz(0, 3, 3)
    adjoint_x(0, 0, 2)
    send_result(0, 0)
    adjoint_x(0, 3, 3)
    send_result(0, 3)
    drain_blocks(0)
    absorb(1, 2)
    absorb(1, 3)
    absorb(1, 1)
    forward_yz(1, 2, 0)
    forward_yz(1, 1, 1)
    forward_x(1, 2, 0)
    forward_x(1, 1, 1)
    adjoint_yz(1, 1, 2)
    absorb(1, 4)
    forward_yz(1, 3, 0)
    adjoint_x(1, 1, 2)
    send_result(1, 1)
    forward_x(1, 3, 0)
    adjoint_yz(1, 2, 3)
    absorb(1, 0)
    forward_yz(1, 0, 1)
    adjoint_x(1, 2, 3)
    send_result(1, 2)
    forward_x(1, 0, 1)
    adjoint_yz(1, 0, 2)
    absorb(1, 5)
    forward_yz(1, 4, 0)
    adjoint_x(1, 0, 2)
    send_result(1, 0)
    forward_x(1, 4, 0)
    adjoint_yz(1, 3, 3)
    adjoint_x(1, 3, 3)
    send_result(1, 3)
    drain_blocks(ITERS - 1)
    for s in range(strips):
        for block in range(blocks):
            part = out_ref.at[:, block * UNIT:(block + 1) * UNIT, s * LANES:(s + 1) * LANES]
            arrived(part, final_recv.at[s, block])
    for block in range(blocks):
        for step in range(1, gz_count):
            final_copy(step, block).wait_send()
        when(jnp.logical_not(at_home), lambda block=block: final_copy(0, block).wait_send())


def by_strips(lat_count, gz_count, tiles, offsets, taps_x, taps_y, taps_z):
    plane_count, tile_rows, width = tiles.shape
    brick = tile_rows - SPILL
    planes = plane_count * gz_count
    groups = planes // (LANES // UNIT)
    blocks = brick // UNIT
    tall, deep = planes * UNIT, planes * 2 * UNIT
    dma = pltpu.SemaphoreType.DMA
    hbm = pl.BlockSpec(memory_space=pltpu.HBM)
    return pl.pallas_call(
        functools.partial(strip_kernel, lat_count, gz_count),
        out_shape=jax.ShapeDtypeStruct((plane_count, brick, width), F32),
        in_specs=[hbm] * 5,
        out_specs=pl.BlockSpec(memory_space=pl.ANY),
        scratch_shapes=[
            pltpu.VMEM(tiles.shape, F32), pltpu.SMEM(offsets.shape, jnp.int32),
            pltpu.SMEM(taps_x.shape, F32), pltpu.SMEM(taps_y.shape, F32),
            pltpu.SMEM(taps_z.shape, F32), dma((5,)),
            pltpu.VMEM((planes, tile_rows + 2 * SPILL, LANES), F32),
            pltpu.VMEM((2, planes, SPILL, LANES), F32),
            pltpu.VMEM((2, planes, SPILL, LANES), F32),
            pltpu.VMEM((planes, brick + 2 * UNIT, 2 * LANES), F32),
            pltpu.VMEM((ITERS - 1, planes, brick + 2 * UNIT, LANES), F32),
            pltpu.VMEM((ITERS, 2, planes, brick + 2 * UNIT, 2 * LANES), BF16),
            pltpu.VMEM((4, 2 * tall, 2 * LANES), BF16),
            pltpu.VMEM((2, planes, brick + UNIT, 2 * LANES), BF16),
            pltpu.VMEM((ITERS, 2, groups, brick, LANES), F32),
            pltpu.VMEM((ITERS, 2, groups, brick + 2 * UNIT, LANES), F32),
            pltpu.VMEM((planes, brick, LANES), F32),
            pltpu.VMEM((2, 2 * LANES, 2 * LANES), BF16),
            pltpu.VMEM((2, 2 * LANES, LANES), BF16),
            pltpu.VMEM((2 * tall, deep), BF16),
            pltpu.VMEM((2 * tall, deep), BF16),
            dma((gz_count, 3)), dma((gz_count, 3)), dma((2,)), dma((2,)),
            dma((ITERS, 2)), dma((ITERS, 2)),
            dma((ITERS, 2, blocks + 2)), dma((ITERS, 2, blocks + 2)),
            dma((gz_count, blocks)), dma((gz_count, blocks)),
        ],
        compiler_params=pltpu.CompilerParams(
            has_side_effects=True, collective_id=0, vmem_limit_bytes=VMEM_LIMIT),
    )(tiles, offsets, taps_x, taps_y, taps_z)


def local(lat_count, gz_count, tiles, offsets, taps_x, taps_y, taps_z):
    plane_count, tile_rows, width = tiles.shape
    brick, planes = tile_rows - SPILL, plane_count * gz_count
    fits = (width == gz_count * LANES and gz_count % 2 == 0 and lat_count % 2 == 0
            and planes % (LANES // UNIT) == 0 and brick % UNIT == 0 and brick >= 4 * UNIT)
    arrange = by_strips if fits else by_rows
    return arrange(lat_count, gz_count, tiles, offsets, taps_x, taps_y, taps_z)


def solution(mesh):
    in_specs = (P("gz", "lat", None), P(), P(), P(), P())
    out_specs = P("gz", "lat", None)
    body = functools.partial(local, mesh.shape["lat"], mesh.shape["gz"])
    return jax.shard_map(body, mesh=mesh, in_specs=in_specs, out_specs=out_specs, check_vma=False)
```

```python
import functools

import jax
import jax.numpy as jnp
from jax import lax
from jax.experimental import pallas as pl
from jax.experimental.pallas import tpu as pltpu
from jax.sharding import PartitionSpec as P

SPILL = 32
ITERS = 2
REACH = 16
CHUNKS = 2
LANES = 128
UNIT = 2 * REACH
VMEM_LIMIT = 60 * 1024 * 1024
MESH = pl.DeviceIdType.MESH
F32 = jnp.float32
BF16 = jnp.bfloat16


def halves(value):
    high = value.astype(BF16)
    return high, (value - high.astype(F32)).astype(BF16)


def product(left, right):
    (left_high, left_low), (right_high, right_low) = left, right

    def dot(a, b):
        return jnp.dot(a, b, preferred_element_type=F32)

    return dot(left_high, right_high) + (dot(left_high, right_low) + dot(left_low, right_high))


def banded(taps_ref, index):
    def add_tap(k, value):
        return jnp.where(index == k, taps_ref[k], value)

    return lax.fori_loop(0, taps_ref.shape[0], add_tap, jnp.zeros(index.shape, F32))


def shifted_rows(value, amount):
    length = value.shape[0]
    amounts = jnp.zeros(value.shape, jnp.int32) + amount
    bit = 1
    while bit <= SPILL:
        moved = pltpu.roll(value, length - bit, 0)
        value = jnp.where((amounts & bit) != 0, moved, value)
        bit *= 2
    return value[: length - SPILL]


def store_halves(ref, where, value):
    high, low = halves(value)
    ref[(0,) + where] = high
    ref[(1,) + where] = low


def kernel(
    lat_count, gz_count,
    tiles_hbm, offsets_hbm, taps_x_hbm, taps_y_hbm, taps_z_hbm, out_ref,
    tiles_ref, offsets_ref, taps_x_ref, taps_y_ref, taps_z_ref, load_sem,
    shifted, gathered, left_spill, right_spill, observed, estimate, ratio, lateral_y, final,
    x_forward, x_adjoint, yz_forward, yz_adjoint,
    tile_send, tile_recv, left_send, left_recv, right_send, right_recv,
    halo_send, halo_recv, final_send, final_recv, local_sem,
):
    lat, gz = lax.axis_index("lat"), lax.axis_index("gz")
    pairs = ((tiles_hbm, tiles_ref), (offsets_hbm, offsets_ref), (taps_x_hbm, taps_x_ref),
             (taps_y_hbm, taps_y_ref), (taps_z_hbm, taps_z_ref))
    loads = [pltpu.make_async_copy(source, target, load_sem.at[i])
             for i, (source, target) in enumerate(pairs)]
    for load in loads:
        load.start()
    plane_count, tile_rows, width = tiles_ref.shape
    slots, planes, rows, _ = observed.shape
    brick = tile_rows - SPILL
    depth = slots // 2
    spill_blocks = SPILL // rows
    units, _, unit, _ = ratio.shape
    out_rows = units * unit
    total = lat_count * gz_count

    chunk = width // CHUNKS
    chunks = [slice(c * chunk, (c + 1) * chunk) for c in range(CHUNKS)]

    def owner(lat_index, block):
        return jnp.where(lat_index % 2 == 0, block, gz_count - 1 - block)

    block = owner(lat, gz)
    place = lat * gz_count + block

    def device_at(position):
        lat_index = position // gz_count
        return lat_index, owner(lat_index, position % gz_count)

    own_planes = pl.ds(gz * plane_count, plane_count)

    def tile_copy(step, c):
        target = (gz + step) % gz_count
        source_rows = pl.ds(pl.multiple_of(owner(lat, target) * rows, rows), rows)
        return pltpu.make_async_remote_copy(
            shifted.at[:, source_rows, chunks[c]], gathered.at[own_planes, :, chunks[c]],
            tile_send.at[step, c], tile_recv.at[step, c], (lat, target), MESH)

    def right_going(q, c):
        return pltpu.make_async_remote_copy(
            tiles_ref.at[:, brick:tile_rows, chunks[c]],
            left_spill.at[own_planes, 0:SPILL, chunks[c]],
            left_send.at[q, c], left_recv.at[gz, c], (lat + 1, owner(lat + 1, q)), MESH)

    def left_going(q, c):
        return pltpu.make_async_remote_copy(
            tiles_ref.at[:, 0:SPILL, chunks[c]],
            right_spill.at[own_planes, SPILL:2 * SPILL, chunks[c]],
            right_send.at[q, c], right_recv.at[gz, c], (lat - 1, owner(lat - 1, gz_count - 1 - q)), MESH)

    has_right, has_left = lat < lat_count - 1, lat > 0
    others = [e for e in range(-depth, depth + 1) if e != 0]

    def there(e):
        return (place + e >= 0) & (place + e < total)

    barrier = pltpu.get_barrier_semaphore()

    def greet(device):
        pl.semaphore_signal(barrier, inc=1, device_id=device, device_id_type=MESH)

    expected = gz_count - 1 + jnp.where(has_right, spill_blocks, 0) + jnp.where(has_left, spill_blocks, 0)
    for step in range(1, gz_count):
        greet((lat, (gz + step) % gz_count))
    for e in others:
        expected = expected + jnp.where(there(e), 1, 0)

        @pl.when(there(e))
        def _():
            greet(device_at(place + e))

    @pl.when(has_left & (block < spill_blocks))
    def _():
        for source in range(gz_count):
            greet((lat - 1, source))

    @pl.when(has_right & (block >= gz_count - spill_blocks))
    def _():
        for source in range(gz_count):
            greet((lat + 1, source))

    loads[0].wait()
    loads[1].wait()
    own_offset = offsets_ref[lat]
    for plane in range(plane_count):
        shifted[plane] = shifted_rows(tiles_ref[plane], 0 - own_offset)
    pl.semaphore_wait(barrier, expected)

    for c in range(CHUNKS):
        @pl.when(has_right)
        def _():
            for q in range(spill_blocks):
                right_going(q, c).start()

        @pl.when(has_left)
        def _():
            for q in range(spill_blocks):
                left_going(q, c).start()

        for step in range(1, gz_count):
            tile_copy(step, c).start()
    own_rows = pl.ds(pl.multiple_of(block * rows, rows), rows)
    gathered[own_planes] = shifted[:, own_rows, :]

    @pl.when(has_left & (block < spill_blocks))
    def _():
        left_spill[:, SPILL:2 * SPILL, :] = jnp.zeros((planes, SPILL, width), F32)

    @pl.when(has_right & (block >= gz_count - spill_blocks))
    def _():
        right_spill[:, 0:SPILL, :] = jnp.zeros((planes, SPILL, width), F32)

    for e in others:
        @pl.when(jnp.logical_not(there(e)))
        def _():
            observed[depth + e] = jnp.zeros(observed.shape[1:], F32)
            estimate[depth + e] = jnp.zeros(estimate.shape[1:], F32)

    for load in loads[2:]:
        load.wait()
    half_xy = (taps_x_ref.shape[0] - 1) // 2
    half_z = (taps_z_ref.shape[0] - 1) // 2
    blocks = width // LANES
    gap = (lax.broadcasted_iota(jnp.int32, (LANES, LANES), 0)
           - lax.broadcasted_iota(jnp.int32, (LANES, LANES), 1))

    def build_x(matrix, sign):
        matrix[...] = jnp.zeros_like(matrix)
        for delta in (-1, 0, 1):
            value = banded(taps_x_ref, half_xy + sign * (gap + delta * LANES))
            for column in range(blocks):
                row = column + delta
                if 0 <= row < blocks:
                    spot = (slice(row * LANES, (row + 1) * LANES),
                            slice(column * LANES, (column + 1) * LANES))
                    store_halves(matrix, spot, value)

    build_x(x_forward, 1)

    def axial(lane_plane, plane, sign):
        weights = jnp.zeros(lane_plane.shape, F32)
        for other in range(planes):
            tap = taps_z_ref[half_z + sign * (other - plane)]
            weights = jnp.where(lane_plane == other, tap, weights)
        return weights

    lanes = lax.broadcasted_iota(jnp.int32, (out_rows, planes * rows), 1)
    out_ids = lax.broadcasted_iota(jnp.int32, (out_rows, planes * rows), 0)
    lane_row = lanes % rows
    lane_plane = (lax.broadcasted_iota(jnp.int32, (8, planes * rows), 1)) // rows

    def reached(slot):
        start = (slot - depth) * rows + REACH - half_xy
        return max(0, start // unit), min(units, (start + rows + 2 * half_xy - 1) // unit + 1)

    def build_axial(z, carry):
        weights = axial(lane_plane, z, 1)[0:1]
        for slot in range(slots):
            block_value = lateral_y[slot] * weights
            for u in range(*reached(slot)):
                spot = (slot, pl.ds(pl.multiple_of((u * planes + z) * unit, unit), unit), slice(None))
                store_halves(yz_forward, spot, block_value[u * unit:(u + 1) * unit])
        return carry

    for slot in range(slots):
        index = lane_row + (slot - depth) * rows - (out_ids - REACH) + half_xy
        lateral_y[slot] = banded(taps_y_ref, index)
    lax.fori_loop(0, planes, build_axial, 0)

    wide = planes * out_rows

    def build_adjoint():
        build_x(x_adjoint, -1)
        lane = lax.broadcasted_iota(jnp.int32, (rows, wide), 1)
        row_ids = lax.broadcasted_iota(jnp.int32, (rows, wide), 0)
        back_lateral = banded(taps_y_ref, half_xy - (lane // (unit * planes) * unit + lane % unit - REACH - row_ids))
        wide_plane = lax.broadcasted_iota(jnp.int32, (8, wide), 1) // unit % planes
        for z in range(planes):
            weights = axial(wide_plane, z, -1)[0:1]
            store_halves(yz_adjoint, (slice(z * rows, (z + 1) * rows), slice(None)), back_lateral * weights)

    left_offset = offsets_ref[jnp.maximum(lat - 1, 0)]
    right_offset = offsets_ref[jnp.minimum(lat + 1, lat_count - 1)]
    brick_rows = block * rows + lax.broadcasted_iota(jnp.int32, (rows, chunk), 0)
    from_left = has_left & (brick_rows < SPILL + left_offset)
    from_right = has_right & (brick_rows >= brick + right_offset)
    counts = 1.0 + jnp.where(from_left, 1.0, 0.0) + jnp.where(from_right, 1.0, 0.0)

    def halo_copy(buffer, which, e, c):
        return pltpu.make_async_remote_copy(
            buffer.at[depth, :, :, chunks[c]], buffer.at[depth - e, :, :, chunks[c]],
            halo_send.at[which, depth - e, c], halo_recv.at[which, depth - e, c],
            device_at(place + e), MESH)

    def send_halos(buffer, which, c):
        for e in others:
            @pl.when(there(e))
            def _():
                halo_copy(buffer, which, e, c).start()

    for c in range(CHUNKS):
        for step in range(1, gz_count):
            tile_copy(step, c).wait_recv()

        @pl.when(has_left & (block < spill_blocks))
        def _():
            for source in range(gz_count):
                sent = slice(source * plane_count, (source + 1) * plane_count)
                part = left_spill.at[sent, 0:SPILL, chunks[c]]
                pltpu.make_async_copy(part, part, left_recv.at[source, c]).wait()
            reach = pl.ds(pl.multiple_of(block * rows, 8), rows + SPILL)
            for z in range(planes):
                spill = left_spill[z, reach, chunks[c]]
                gathered[z, :, chunks[c]] += shifted_rows(spill, 0 - left_offset)

        @pl.when(has_right & (block >= gz_count - spill_blocks))
        def _():
            for source in range(gz_count):
                sent = slice(source * plane_count, (source + 1) * plane_count)
                part = right_spill.at[sent, SPILL:2 * SPILL, chunks[c]]
                pltpu.make_async_copy(part, part, right_recv.at[source, c]).wait()
            first = (block - (gz_count - spill_blocks)) * rows
            reach = pl.ds(pl.multiple_of(first, 8), rows + SPILL)
            for z in range(planes):
                spill = right_spill[z, reach, chunks[c]]
                gathered[z, :, chunks[c]] += shifted_rows(spill, 0 - right_offset)

        for z in range(planes):
            observed[depth, z, :, chunks[c]] = gathered[z, :, chunks[c]] / counts
        send_halos(observed, 0, c)

    build_adjoint()

    def final_copy(step, c):
        target = (gz + step) % gz_count
        return pltpu.make_async_remote_copy(
            final.at[pl.ds(target * plane_count, plane_count), :, chunks[c]],
            out_ref.at[:, own_rows, chunks[c]],
            final_send.at[step, c], final_recv.at[step, c], (lat, target), MESH)

    for which, buffer in zip(range(ITERS), [observed] + [estimate] * (ITERS - 1)):
        def part(slot, c):
            first, last = reached(slot)
            spot = slice(first * planes * unit, last * planes * unit)
            data = halves(buffer[slot, :, :, chunks[c]].reshape(planes * rows, chunk))
            value = product((yz_forward[0, slot, spot], yz_forward[1, slot, spot]), data)
            return {u: value[(u - first) * planes * unit:(u + 1 - first) * planes * unit]
                    for u in range(first, last)}

        sums = [part(depth, c) for c in range(CHUNKS)]
        blurred = None
        for c in range(CHUNKS):
            lateral = sums[c]
            for e in others:
                @pl.when(there(e))
                def _():
                    halo_copy(buffer, which, 0 - e, c).wait_recv()
                for u, value in part(depth + e, c).items():
                    lateral[u] = lateral[u] + value if u in lateral else value
            lateral = jnp.concatenate([lateral[u] for u in range(units)], 0)
            term = product(halves(lateral), (x_forward[0, chunks[c], :], x_forward[1, chunks[c], :]))
            blurred = term if blurred is None else blurred + term
        blurred = blurred.reshape(units, planes, unit, width)
        for u in range(units):
            row = u * unit - REACH + depth * rows
            slot, first = row // rows, row % rows
            quotient = observed[slot, :, first:first + unit, :] / blurred[u]
            ratio[u] = jnp.where(there(slot - depth), quotient, 0.0)
        data = halves(ratio[...].reshape(wide, width))
        back = halves(product((yz_adjoint[0], yz_adjoint[1]), data))
        for c in range(CHUNKS):
            gain = product(back, (x_adjoint[0, :, chunks[c]], x_adjoint[1, :, chunks[c]]))
            value = buffer[depth, :, :, chunks[c]] * gain.reshape(planes, rows, chunk)
            if which < ITERS - 1:
                estimate[depth, :, :, chunks[c]] = value
                send_halos(estimate, which + 1, c)
            else:
                final[:, :, chunks[c]] = value
                for step in range(1, gz_count):
                    final_copy(step, c).start()

    mine = pltpu.make_async_copy(final.at[own_planes], out_ref.at[:, own_rows, :], local_sem)
    mine.start()

    for c in range(CHUNKS):
        for step in range(1, gz_count):
            tile_copy(step, c).wait_send()

        @pl.when(has_right)
        def _():
            for q in range(spill_blocks):
                right_going(q, c).wait_send()

        @pl.when(has_left)
        def _():
            for q in range(spill_blocks):
                left_going(q, c).wait_send()

        for which, buffer in zip(range(ITERS), [observed] + [estimate] * (ITERS - 1)):
            for e in others:
                @pl.when(there(e))
                def _():
                    halo_copy(buffer, which, e, c).wait_send()

        for step in range(1, gz_count):
            final_copy(step, c).wait()
    mine.wait()


def by_rows(lat_count, gz_count, tiles, offsets, taps_x, taps_y, taps_z):
    plane_count, tile_rows, width = tiles.shape
    brick = tile_rows - SPILL
    rows = brick // gz_count
    planes = plane_count * gz_count
    depth = 2 * REACH // rows
    slots = 2 * depth + 1
    out_rows = rows + 2 * REACH
    unit = 16 if rows % 16 == 0 else 8
    spill_blocks = SPILL // rows
    dma = pltpu.SemaphoreType.DMA
    hbm = pl.BlockSpec(memory_space=pltpu.HBM)
    return pl.pallas_call(
        functools.partial(kernel, lat_count, gz_count),
        out_shape=jax.ShapeDtypeStruct((plane_count, brick, width), F32),
        in_specs=[hbm] * 5,
        out_specs=pl.BlockSpec(memory_space=pl.ANY),
        scratch_shapes=[
            pltpu.VMEM(tiles.shape, F32), pltpu.SMEM(offsets.shape, jnp.int32),
            pltpu.SMEM(taps_x.shape, F32), pltpu.SMEM(taps_y.shape, F32),
            pltpu.SMEM(taps_z.shape, F32), dma((5,)),
            pltpu.VMEM((plane_count, brick, width), F32),
            pltpu.VMEM((planes, rows, width), F32),
            pltpu.VMEM((planes, 2 * SPILL, width), F32),
            pltpu.VMEM((planes, 2 * SPILL, width), F32),
            pltpu.VMEM((slots, planes, rows, width), F32),
            pltpu.VMEM((slots, planes, rows, width), F32),
            pltpu.VMEM((out_rows // unit, planes, unit, width), F32),
            pltpu.VMEM((slots, out_rows, planes * rows), F32),
            pltpu.VMEM((planes, rows, width), F32),
            pltpu.VMEM((2, width, width), BF16),
            pltpu.VMEM((2, width, width), BF16),
            pltpu.VMEM((2, slots, planes * out_rows, planes * rows), BF16),
            pltpu.VMEM((2, planes * rows, planes * out_rows), BF16),
            dma((gz_count, CHUNKS)), dma((gz_count, CHUNKS)),
            dma((spill_blocks, CHUNKS)), dma((gz_count, CHUNKS)),
            dma((spill_blocks, CHUNKS)), dma((gz_count, CHUNKS)),
            dma((ITERS, slots, CHUNKS)), dma((ITERS, slots, CHUNKS)),
            dma((gz_count, CHUNKS)), dma((gz_count, CHUNKS)), dma,
        ],
        compiler_params=pltpu.CompilerParams(
            has_side_effects=True, collective_id=0, vmem_limit_bytes=60 * 1024 * 1024),
    )(tiles, offsets, taps_x, taps_y, taps_z)


def column_of(lane, outside):
    left, right = LANES + UNIT, LANES + 2 * UNIT
    return jnp.where(lane < LANES, lane,
                     jnp.where(lane < left, lane - left, jnp.where(lane < right, lane - UNIT, outside)))


def strip_kernel(
    lat_count, gz_count,
    tiles_hbm, offsets_hbm, taps_x_hbm, taps_y_hbm, taps_z_hbm, out_ref,
    tiles_ref, offsets_ref, taps_x_ref, taps_y_ref, taps_z_ref, load_sem,
    raw, spill_out, spill_in, observed, estimate, parts, middle, quotient, edges, halo, final,
    x_forward, x_adjoint, yz_forward, yz_adjoint,
    tile_send, tile_recv, spill_send, spill_recv, row_send, row_recv,
    side_send, side_recv, final_send, final_recv,
):
    lat, gz = lax.axis_index("lat"), lax.axis_index("gz")
    pairs = ((tiles_hbm, tiles_ref), (offsets_hbm, offsets_ref), (taps_x_hbm, taps_x_ref),
             (taps_y_hbm, taps_y_ref), (taps_z_hbm, taps_z_ref))
    loads = [pltpu.make_async_copy(source, target, load_sem.at[i])
             for i, (source, target) in enumerate(pairs)]
    for load in loads:
        load.start()
    plane_count, tile_rows, width = tiles_ref.shape
    planes, brick, _ = final.shape
    blocks = brick // UNIT
    strips = gz_count
    groups = edges.shape[2]
    pack = planes // groups
    lane_x, core = lat % 2, gz % 2
    brick_id = lat - lane_x + core
    strip = jnp.where(lane_x == 0, gz // 2, strips - 1 - gz // 2)
    at_home = core == lane_x

    def device(brick_index, s):
        column = jnp.where(s < strips // 2, 0, 1)
        row = jnp.where(s < strips // 2, s, strips - 1 - s)
        return brick_index - brick_index % 2 + column, 2 * row + brick_index % 2

    has_up, has_down = brick_id > 0, brick_id < lat_count - 1
    has_left, has_right = strip > 0, strip < strips - 1
    vertical = {-1: has_up, 1: has_down}
    sideways = {-1: has_left, 1: has_right}

    def when(condition, action):
        pl.when(condition)(action)

    barrier = pltpu.get_barrier_semaphore()

    def greet(target):
        pl.semaphore_signal(barrier, inc=1, device_id=target, device_id_type=MESH)

    for step in range(1, 2 * gz_count):
        position = (lane_x * gz_count + gz + step) % (2 * gz_count)
        greet((lat - lane_x + position // gz_count, position % gz_count))
    expected = 2 * gz_count - 1
    outward = jnp.where(core == 0, -1, 1)
    has_outward = jnp.where(core == 0, brick_id, lat_count - 1 - brick_id) > 0
    for shift in (-1, 0, 1):
        condition = has_outward if shift == 0 else has_outward & sideways[shift]
        expected = expected + jnp.where(condition, 1, 0)
        when(condition, lambda shift=shift: greet(device(brick_id + outward, strip + shift)))

    side_rows = [slice(q * UNIT, (q + 1) * UNIT) for q in range(blocks + 2)]

    def clear_up():
        spill_in[0] = jnp.zeros(spill_in.shape[1:], F32)
        observed[:, side_rows[0], 0:LANES] = jnp.zeros((planes, UNIT, LANES), F32)
        estimate[:, :, side_rows[0], :] = jnp.zeros((ITERS - 1, planes, UNIT, LANES), F32)
        halo[:, :, :, side_rows[0], :] = jnp.zeros((ITERS, 2, groups, UNIT, LANES), F32)

    def clear_down():
        spill_in[1] = jnp.zeros(spill_in.shape[1:], F32)
        observed[:, side_rows[-1], 0:LANES] = jnp.zeros((planes, UNIT, LANES), F32)
        estimate[:, :, side_rows[-1], :] = jnp.zeros((ITERS - 1, planes, UNIT, LANES), F32)
        halo[:, :, :, side_rows[-1], :] = jnp.zeros((ITERS, 2, groups, UNIT, LANES), F32)

    def clear_side(side):
        halo[:, side] = jnp.zeros((ITERS, *halo.shape[2:]), F32)

    when(jnp.logical_not(has_up), clear_up)
    when(jnp.logical_not(has_down), clear_down)
    when(jnp.logical_not(has_left), lambda: clear_side(0))
    when(jnp.logical_not(has_right), lambda: clear_side(1))
    raw[:, 0:SPILL, :] = jnp.zeros((planes, SPILL, LANES), F32)
    raw[:, SPILL + tile_rows:, :] = jnp.zeros((planes, SPILL, LANES), F32)

    pieces = (slice(0, SPILL), slice(brick, tile_rows), slice(SPILL, brick))
    own_planes = pl.ds(gz * plane_count, plane_count)

    def lanes_of(s):
        return pl.ds(pl.multiple_of(s * LANES, LANES), LANES)

    def landed(piece):
        return slice(SPILL + piece.start, SPILL + piece.stop)

    def tile_copy(step, i):
        s = (strip + step) % strips
        return pltpu.make_async_remote_copy(
            tiles_ref.at[:, pieces[i], lanes_of(s)], raw.at[own_planes, landed(pieces[i]), :],
            tile_send.at[step, i], tile_recv.at[gz, i], device(lat, s), MESH)

    def tile_stay(i):
        return pltpu.make_async_copy(
            tiles_ref.at[:, pieces[i], lanes_of(strip)], raw.at[own_planes, landed(pieces[i]), :],
            tile_recv.at[gz, i])

    def arrived(part, semaphore):
        pltpu.make_async_copy(part, part, semaphore).wait()

    def tile_wait(i):
        for source in range(gz_count):
            sent = slice(source * plane_count, (source + 1) * plane_count)
            arrived(raw.at[sent, landed(pieces[i]), :], tile_recv.at[source, i])

    def send_tiles(steps, numbers):
        for i in numbers:
            for step in steps:
                if step > 0:
                    tile_copy(step, i).start()
                else:
                    when(at_home, lambda i=i: tile_stay(i).start())
                    when(jnp.logical_not(at_home), lambda i=i: tile_copy(0, i).start())

    loads[0].wait()
    pl.semaphore_wait(barrier, expected)
    send_tiles((*range(1, strips), 0), range(len(pieces)))

    for load in loads[1:]:
        load.wait()
    half_x = (taps_x_ref.shape[0] - 1) // 2
    half_y = (taps_y_ref.shape[0] - 1) // 2
    half_z = (taps_z_ref.shape[0] - 1) // 2
    far = 1 << 20

    def build_x(matrix, sign):
        _, depth, breadth = matrix.shape
        tall = LANES // 2
        for start in range(0, depth, tall):
            inner = start + lax.broadcasted_iota(jnp.int32, (tall, breadth), 0)
            outer = lax.broadcasted_iota(jnp.int32, (tall, breadth), 1)
            gap = column_of(inner, far) - column_of(outer, 0 - far)
            high, low = halves(banded(taps_x_ref, half_x + sign * gap))
            matrix[0, start:start + tall, :] = high
            matrix[1, start:start + tall, :] = low

    tall, deep = planes * UNIT, planes * 2 * UNIT

    def build_yz(matrix, sign):
        lane = lax.broadcasted_iota(jnp.int32, (UNIT, deep), 1)
        row = lax.broadcasted_iota(jnp.int32, (UNIT, deep), 0)
        lateral = banded(taps_y_ref, half_y + sign * (lane % (2 * UNIT) - row) - REACH * sign)
        lane_plane = lax.broadcasted_iota(jnp.int32, (8, deep), 1) // (2 * UNIT)
        for z in range(planes):
            weights = jnp.zeros(lane_plane.shape, F32)
            for other in range(planes):
                weights = jnp.where(lane_plane == other, taps_z_ref[half_z + sign * (other - z)], weights)
            high, low = halves(lateral * weights[0:1])
            matrix[z * UNIT:(z + 1) * UNIT, :] = high
            matrix[tall + z * UNIT:tall + (z + 1) * UNIT, :] = low

    build_x(x_forward, 1)
    build_yz(yz_forward, 1)

    own_offset = offsets_ref[brick_id]
    up_offset = offsets_ref[jnp.maximum(brick_id - 1, 0)]
    down_offset = offsets_ref[jnp.minimum(brick_id + 1, lat_count - 1)]

    def spill_copy(i):
        return pltpu.make_async_remote_copy(
            spill_out.at[i], spill_in.at[1 - i], spill_send.at[i], spill_recv.at[1 - i],
            device(brick_id + 2 * i - 1, strip), MESH)

    def placed(first):
        return [shifted_rows(raw[z, first:first + UNIT + SPILL, :], 0 - own_offset) for z in range(planes)]

    for i, condition in enumerate((has_up, has_down)):
        tile_wait(i)
        for z, value in enumerate(placed(i * (tile_rows))):
            spill_out[i, z] = value
        when(condition, lambda i=i: spill_copy(i).start())

    lane_ids = lax.broadcasted_iota(jnp.int32, (UNIT, LANES), 1)

    def current(which):
        return observed if which == 0 else estimate.at[which - 1]

    def row_copy(which, way):
        source = side_rows[1] if way < 0 else side_rows[blocks]
        target = side_rows[blocks + 1] if way < 0 else side_rows[0]
        i = (way + 1) // 2
        buffer = current(which)
        return pltpu.make_async_remote_copy(
            buffer.at[:, source, 0:LANES], buffer.at[:, target, 0:LANES],
            row_send.at[which, i], row_recv.at[which, i], device(brick_id + way, strip), MESH)

    def side_copy(which, shift, way, block):
        side = (1 - shift) // 2
        q = block + 1 if way == 0 else (blocks + 1 if way < 0 else 0)
        return pltpu.make_async_remote_copy(
            edges.at[which, side, :, block * UNIT:(block + 1) * UNIT, :],
            halo.at[which, side, :, side_rows[q], :],
            side_send.at[which, side, q], side_recv.at[which, side, q],
            device(brick_id + way, strip + shift), MESH)

    def all_copies(which, block):
        ways = ([-1] if block == 0 else []) + ([1] if block == blocks - 1 else [])
        copies = [(sideways[shift], side_copy(which, shift, 0, block)) for shift in (1, -1)]
        for way in ways:
            for shift in (1, -1):
                copies.append((sideways[shift] & vertical[way], side_copy(which, shift, way, block)))
            copies.append((vertical[way], row_copy(which, way)))
        return copies

    def keep(which, block, values):
        rows = side_rows[block + 1]
        spot = slice(block * UNIT, (block + 1) * UNIT)
        buffer = current(which)
        for group in range(groups):
            right = left = None
            for j in range(pack):
                z = group * pack + j
                value = values[z]
                buffer[z, rows, 0:LANES] = value
                store_halves(parts.at[which], (z, rows, slice(0, LANES)), value)
                moved = pltpu.roll(value, (UNIT * (j + 1)) % LANES, 1) if j + 1 < pack else value
                right = moved if right is None else jnp.where(lane_ids // UNIT == j, moved, right)
                moved = pltpu.roll(value, UNIT * j, 1) if j > 0 else value
                left = moved if left is None else jnp.where(lane_ids // UNIT == j, moved, left)
            edges[which, 0, group, spot, :] = right
            edges[which, 1, group, spot, :] = left

    def send_block(which, block):
        for condition, copy in all_copies(which, block):
            when(condition, lambda copy=copy: copy.start())

    def absorb(which, q):
        rows = side_rows[q]
        way = -1 if q == 0 else (1 if q == blocks + 1 else 0)
        buffer = current(which)
        if way != 0:
            when(vertical[way], lambda: arrived(buffer.at[:, rows, 0:LANES], row_recv.at[which, (1 - way) // 2]))
            for z in range(planes):
                store_halves(parts.at[which], (z, rows, slice(0, LANES)), buffer[z, rows, 0:LANES])
        for side, condition in enumerate((has_left, has_right)):
            condition = condition if way == 0 else condition & vertical[way]
            when(condition, lambda side=side: arrived(
                halo.at[which, side, :, rows, :], side_recv.at[which, side, q]))
        for group in range(groups):
            from_left, from_right = halo[which, 0, group, rows, :], halo[which, 1, group, rows, :]
            for j in range(pack):
                z = group * pack + j
                left = pltpu.roll(from_left, LANES - UNIT * j, 1) if j > 0 else from_left
                right = pltpu.roll(from_right, (LANES + UNIT - UNIT * j) % LANES, 1) if j != 1 else from_right
                value = jnp.where(lane_ids < UNIT, left, jnp.where(lane_ids < 2 * UNIT, right, 0.0))
                if which == 0:
                    observed[z, rows, LANES:2 * LANES] = value
                store_halves(parts.at[which], (z, rows, slice(LANES, 2 * LANES)), value)

    def dot(a, b):
        return jnp.dot(a, b, preferred_element_type=F32)

    def apply_yz(matrix, data_ref, first, slot):
        high, low = [data_ref[i, :, first:first + 2 * UNIT, :].reshape(deep, 2 * LANES) for i in (0, 1)]
        both = dot(matrix[...], high)
        value = both[:tall] + (both[tall:] + dot(matrix[:tall, :], low))
        middle[slot, :tall, :], middle[slot, tall:, :] = halves(value)

    def apply_x(matrix, slot):
        both = dot(middle[slot], matrix[0])
        return both[:tall] + (both[tall:] + dot(middle[slot, :tall, :], matrix[1]))

    wide_lane = lax.broadcasted_iota(jnp.int32, (UNIT, 2 * LANES), 1)
    wide_row = lax.broadcasted_iota(jnp.int32, (UNIT, 2 * LANES), 0)
    inside_columns = ((wide_lane < LANES)
                      | (has_left & (wide_lane >= LANES) & (wide_lane < LANES + UNIT))
                      | (has_right & (wide_lane >= LANES + UNIT) & (wide_lane < LANES + 2 * UNIT)))

    def forward_yz(which, k, slot):
        apply_yz(yz_forward, parts.at[which], k * UNIT, slot)

    def forward_x(which, k, slot):
        blurred = apply_x(x_forward, slot)
        inside = inside_columns
        if k == 0:
            inside = inside & (has_up | (wide_row >= REACH))
        if k == blocks:
            inside = inside & (has_down | (wide_row < UNIT - REACH))
        for z in range(planes):
            start = k * UNIT + UNIT - REACH
            value = observed[z, start:start + UNIT, :] / blurred[z * UNIT:(z + 1) * UNIT]
            store_halves(quotient, (z, slice(k * UNIT, (k + 1) * UNIT), slice(None)),
                         jnp.where(inside, value, 0.0))

    def final_copy(step, block):
        target = (gz + step) % gz_count
        rows = slice(block * UNIT, (block + 1) * UNIT)
        return pltpu.make_async_remote_copy(
            final.at[pl.ds(target * plane_count, plane_count), rows, :],
            out_ref.at[:, rows, lanes_of(strip)],
            final_send.at[step, block], final_recv.at[strip, block], (brick_id, target), MESH)

    def final_stay(block):
        rows = slice(block * UNIT, (block + 1) * UNIT)
        return pltpu.make_async_copy(
            final.at[own_planes, rows, :], out_ref.at[:, rows, lanes_of(strip)], final_recv.at[strip, block])

    def adjoint_yz(which, block, slot):
        apply_yz(yz_adjoint, quotient, block * UNIT, slot)

    def adjoint_x(which, block, slot):
        gain = apply_x(x_adjoint, slot)
        buffer = current(which)
        values = [buffer[z, side_rows[block + 1], 0:LANES] * gain[z * UNIT:(z + 1) * UNIT] for z in range(planes)]
        if which < ITERS - 1:
            keep(which + 1, block, values)
            return
        for z in range(planes):
            final[z, block * UNIT:(block + 1) * UNIT, :] = values[z]

    def send_result(which, block):
        if which < ITERS - 1:
            send_block(which + 1, block)
            return
        for step in range(1, gz_count):
            final_copy(step, block).start()
        when(at_home, lambda: final_stay(block).start())
        when(jnp.logical_not(at_home), lambda: final_copy(0, block).start())

    build_x(x_adjoint, -1)
    build_yz(yz_adjoint, -1)
    tile_wait(len(pieces) - 1)
    inner = list(range(1, blocks - 1))
    row_ids = lax.broadcasted_iota(jnp.int32, (UNIT, LANES), 0)

    def drain_tiles():
        for i in range(len(pieces)):
            for step in range(1, strips):
                tile_copy(step, i).wait_send()
            when(jnp.logical_not(at_home), lambda i=i: tile_copy(0, i).wait_send())
        for i, condition in enumerate((has_up, has_down)):
            when(condition, lambda i=i: spill_copy(i).wait_send())

    def drain_blocks(which):
        for block in range(blocks):
            for condition, copy in all_copies(which, block):
                when(condition, lambda copy=copy: copy.wait_send())

    def start_block(block):
        values = placed(SPILL + block * UNIT)
        for i, (edge, condition) in enumerate(((0, has_up), (blocks - 1, has_down))):
            if block == edge:
                when(condition, lambda i=i: arrived(spill_in.at[i], spill_recv.at[i]))
                limit = SPILL + up_offset - block * UNIT if i == 0 else brick + down_offset - block * UNIT
                shared = has_up & (row_ids < limit) if i == 0 else has_down & (row_ids >= limit)
                counts = jnp.where(shared, 2.0, 1.0)
                values = [(value + spill_in[i, z]) / counts for z, value in enumerate(values)]
        keep(0, block, values)
        send_block(0, block)

    start_block(1)
    start_block(2)
    start_block(0)
    start_block(3)
    drain_tiles()
    absorb(0, 2)
    absorb(0, 3)
    absorb(0, 1)
    absorb(0, 4)
    forward_yz(0, 2, 0)
    forward_yz(0, 1, 1)
    forward_x(0, 2, 0)
    forward_yz(0, 3, 0)
    forward_x(0, 1, 1)
    adjoint_yz(0, 1, 2)
    forward_x(0, 3, 0)
    adjoint_yz(0, 2, 3)
    adjoint_x(0, 1, 2)
    adjoint_x(0, 2, 3)
    send_result(0, 1)
    send_result(0, 2)
    absorb(0, 0)
    absorb(0, 5)
    forward_yz(0, 0, 1)
    forward_yz(0, 4, 0)
    forward_x(0, 0, 1)
    forward_x(0, 4, 0)
    adjoint_yz(0, 0, 2)
    adjoint_yz(0, 3, 3)
    adjoint_x(0, 0, 2)
    send_result(0, 0)
    adjoint_x(0, 3, 3)
    send_result(0, 3)
    drain_blocks(0)
    absorb(1, 2)
    absorb(1, 3)
    absorb(1, 1)
    forward_yz(1, 2, 0)
    forward_yz(1, 1, 1)
    forward_x(1, 2, 0)
    forward_x(1, 1, 1)
    adjoint_yz(1, 1, 2)
    absorb(1, 4)
    forward_yz(1, 3, 0)
    adjoint_x(1, 1, 2)
    send_result(1, 1)
    forward_x(1, 3, 0)
    adjoint_yz(1, 2, 3)
    absorb(1, 0)
    forward_yz(1, 0, 1)
    adjoint_x(1, 2, 3)
    send_result(1, 2)
    forward_x(1, 0, 1)
    adjoint_yz(1, 0, 2)
    absorb(1, 5)
    forward_yz(1, 4, 0)
    adjoint_x(1, 0, 2)
    send_result(1, 0)
    forward_x(1, 4, 0)
    adjoint_yz(1, 3, 3)
    adjoint_x(1, 3, 3)
    send_result(1, 3)
    drain_blocks(ITERS - 1)
    for s in range(strips):
        for block in range(blocks):
            part = out_ref.at[:, block * UNIT:(block + 1) * UNIT, s * LANES:(s + 1) * LANES]
            arrived(part, final_recv.at[s, block])
    for block in range(blocks):
        for step in range(1, gz_count):
            final_copy(step, block).wait_send()
        when(jnp.logical_not(at_home), lambda block=block: final_copy(0, block).wait_send())


def by_strips(lat_count, gz_count, tiles, offsets, taps_x, taps_y, taps_z):
    plane_count, tile_rows, width = tiles.shape
    brick = tile_rows - SPILL
    planes = plane_count * gz_count
    groups = planes // (LANES // UNIT)
    blocks = brick // UNIT
    tall, deep = planes * UNIT, planes * 2 * UNIT
    dma = pltpu.SemaphoreType.DMA
    hbm = pl.BlockSpec(memory_space=pltpu.HBM)
    return pl.pallas_call(
        functools.partial(strip_kernel, lat_count, gz_count),
        out_shape=jax.ShapeDtypeStruct((plane_count, brick, width), F32),
        in_specs=[hbm] * 5,
        out_specs=pl.BlockSpec(memory_space=pl.ANY),
        scratch_shapes=[
            pltpu.VMEM(tiles.shape, F32), pltpu.SMEM(offsets.shape, jnp.int32),
            pltpu.SMEM(taps_x.shape, F32), pltpu.SMEM(taps_y.shape, F32),
            pltpu.SMEM(taps_z.shape, F32), dma((5,)),
            pltpu.VMEM((planes, tile_rows + 2 * SPILL, LANES), F32),
            pltpu.VMEM((2, planes, SPILL, LANES), F32),
            pltpu.VMEM((2, planes, SPILL, LANES), F32),
            pltpu.VMEM((planes, brick + 2 * UNIT, 2 * LANES), F32),
            pltpu.VMEM((ITERS - 1, planes, brick + 2 * UNIT, LANES), F32),
            pltpu.VMEM((ITERS, 2, planes, brick + 2 * UNIT, 2 * LANES), BF16),
            pltpu.VMEM((4, 2 * tall, 2 * LANES), BF16),
            pltpu.VMEM((2, planes, brick + UNIT, 2 * LANES), BF16),
            pltpu.VMEM((ITERS, 2, groups, brick, LANES), F32),
            pltpu.VMEM((ITERS, 2, groups, brick + 2 * UNIT, LANES), F32),
            pltpu.VMEM((planes, brick, LANES), F32),
            pltpu.VMEM((2, 2 * LANES, 2 * LANES), BF16),
            pltpu.VMEM((2, 2 * LANES, LANES), BF16),
            pltpu.VMEM((2 * tall, deep), BF16),
            pltpu.VMEM((2 * tall, deep), BF16),
            dma((gz_count, 3)), dma((gz_count, 3)), dma((2,)), dma((2,)),
            dma((ITERS, 2)), dma((ITERS, 2)),
            dma((ITERS, 2, blocks + 2)), dma((ITERS, 2, blocks + 2)),
            dma((gz_count, blocks)), dma((gz_count, blocks)),
        ],
        compiler_params=pltpu.CompilerParams(
            has_side_effects=True, collective_id=0, vmem_limit_bytes=VMEM_LIMIT),
    )(tiles, offsets, taps_x, taps_y, taps_z)


def local(lat_count, gz_count, tiles, offsets, taps_x, taps_y, taps_z):
    plane_count, tile_rows, width = tiles.shape
    brick, planes = tile_rows - SPILL, plane_count * gz_count
    fits = (width == gz_count * LANES and gz_count % 2 == 0 and lat_count % 2 == 0
            and planes % (LANES // UNIT) == 0 and brick % UNIT == 0 and brick >= 4 * UNIT)
    arrange = by_strips if fits else by_rows
    return arrange(lat_count, gz_count, tiles, offsets, taps_x, taps_y, taps_z)


def solution(mesh):
    in_specs = (P("gz", "lat", None), P(), P(), P(), P())
    out_specs = P("gz", "lat", None)
    body = functools.partial(local, mesh.shape["lat"], mesh.shape["gz"])
    return jax.shard_map(body, mesh=mesh, in_specs=in_specs, out_specs=out_specs, check_vma=False)
```
